512 devices in a mesh: dp: 8 (over x, core), section: 4 (over z_lo), seq: 16 (over z_hi, y).
Axes of the slice: x: 4, y: 8, z: 8 (z_hi: 2, z_lo: 4; z = z_hi * 4 + z_lo), core: 2. Of those that a mesh axis runs over, the one named last changes fastest.
Arguments:
- section_inputs: bfloat16 [4, 3, 8, 2048, 768], P('section', None, 'dp', 'seq'), may hold values from -6 to 6
- cotangent: bfloat16 [3, 8, 2048, 768], P(None, 'dp', 'seq'), may hold values from -6 to 6
- conv_weight: bfloat16 [4, 3, 768, 384], P('section'), may hold values from -0.125 to 0.125
- out_weight: bfloat16 [4, 384, 768], P('section'), may hold values from -0.3125 to 0.3125
- norm_scale: float32 [4, 768], P('section'), may hold values from 0.25 to 1.75
- norm_shift: float32 [4, 768], P('section'), may hold values from -3 to 3
- inner_scale: float32 [4, 384], P('section'), may hold values from 0.25 to 1.75
- inner_shift: float32 [4, 384], P('section'), may hold values from -3 to 3
Outputs:
- grad_in: bfloat16 [4, 3, 8, 2048, 768], P('section', None, 'dp', 'seq')
- grad_conv: float32 [4, 3, 768, 384], P('section', None, 'seq')
- grad_out: float32 [4, 384, 768], P('section', None, 'seq')
The draws below stay inside these ranges and needn't reach their ends.
All inputs are finite; a program needn't handle non-finite values.
Results may differ from the reference program's by a relative error of at most 0.025.
Values may be sent and summed in bfloat16 or wider, within the bound.
A program may use at most 64 MiB of HBM per device.

```python
import jax
import jax.numpy as jnp
from jax import lax

C = 768
I = 384
P_DEV = 128
MICRO = 3
BASE_DILATION = 32
SECTIONS = 4
WINDOWS = 8
LENGTH = 2048
N_SEQ = 16


def strengthened(array, rng, source, target, blocks, factor):
    def block_of(axis_at):
        return (jnp.arange(array.shape[axis_at]) // (array.shape[axis_at] // blocks)).reshape((-1,) + (1,) * (array.ndim - 1 - axis_at))

    near = jax.random.permutation(rng, blocks)[block_of(target)]
    other_side = (block_of(target) + blocks // 2) % blocks
    return jnp.where((block_of(source) == near) | (block_of(source) == other_side), factor * array, array)


def levels(own_key, extent, shards, low, top_value):
    level, own = 1.0, jax.random.fold_in(own_key, 6)
    for position, blocks in shards:
        steps = jnp.exp(jax.random.uniform(jax.random.fold_in(own, position), (blocks,), jnp.float32, low / len(shards), top_value / len(shards)))
        level = level * jnp.repeat(steps, extent[position] // blocks).reshape([-1 if axis == position else 1 for axis in range(len(extent))])
    return level


def normal_values(stream_key, dims, width, limit, pieces=(), kind=jnp.bfloat16):
    array = jax.random.normal(stream_key, dims, jnp.float32) * width
    if len(pieces) > 0:
        array = levels(stream_key, dims, pieces, -0.22, 0.18) * array
    return jnp.clip(array, min=-limit, max=limit).astype(kind)


def gaussian_with(own_key, dims, spread, limit, split, heavy, held_as=jnp.bfloat16):
    entries = spread * jax.random.normal(own_key, dims, jnp.float32)
    if split:
        entries = entries * levels(own_key, dims, split, -0.22, 0.18)
    return jnp.clip(strengthened(entries, jax.random.fold_in(own_key, 3), *heavy), -limit, limit).astype(held_as)


def setup_inputs(seed: int = 0) -> dict:
    arg_keys = jax.random.split(jax.random.key(seed), 9)
    return {
        "section_inputs": normal_values(arg_keys[0], (SECTIONS, MICRO, WINDOWS, LENGTH, C), 1.0, 6.0, ((0, 4), (2, 8), (3, 16))),
        "cotangent": gaussian_with(arg_keys[1], (MICRO, WINDOWS, LENGTH, C), 1.0, 6.0, ((1, 8), (2, 16)), (2, 3, 16, 2.0)),
        "conv_weight": normal_values(arg_keys[2], (SECTIONS, 3, C, I), (3 * C) ** -0.5, 0.125, ((0, 4),)),
        "out_weight": normal_values(arg_keys[3], (SECTIONS, I, C), I ** -0.5, 0.3125, ((0, 4),)),
        "norm_scale": jnp.clip(1.0 + 0.15 * jax.random.normal(arg_keys[4], (SECTIONS, C), jnp.float32), 0.25, 1.75),
        "norm_shift": normal_values(arg_keys[5], (SECTIONS, C), 0.5, 3.0, ((0, 4),), jnp.float32),
        "inner_scale": jnp.clip(1.0 + 0.15 * jax.random.normal(arg_keys[6], (SECTIONS, I), jnp.float32), 0.25, 1.75),
        "inner_shift": normal_values(arg_keys[7], (SECTIONS, I), 0.5, 3.0, ((0, 4),), jnp.float32),
    }


gelu_coeff = 0.7978845608028654
cubic_coeff = 0.044715


def gelu_pair(inputs):
    inner_arg = gelu_coeff * (inputs + cubic_coeff * inputs * inputs * inputs)
    tanh_val = jnp.tanh(inner_arg)
    result = 0.5 * inputs * (1.0 + tanh_val)
    slope_val = 0.5 * (1.0 + tanh_val) + 0.5 * inputs * (1.0 - tanh_val * tanh_val) * gelu_coeff * (1.0 + 3.0 * cubic_coeff * inputs * inputs)
    return result, slope_val


def round_trip(values):
    return lax.optimization_barrier(values.astype(jnp.bfloat16)).astype(jnp.float32)


def section_backward(block_in, grad_top, convolution_kernel, out_w, scale_one, shift_one, scale_two, shift_two, dilation_rate):
    channels = block_in.shape[-1]
    inner_width = convolution_kernel.shape[2]
    pre_norm = block_in.astype(jnp.float32) * scale_one + shift_one
    act_val, act_slope = gelu_pair(pre_norm)
    hidden = act_val.astype(jnp.bfloat16)
    padded = jnp.pad(hidden, ((0, 0), (0, 0), (dilation_rate, dilation_rate), (0, 0)))
    tap_rows = jnp.concatenate([padded[:, :, tap_number * dilation_rate: tap_number * dilation_rate + LENGTH] for tap_number in range(3)], axis=3)
    conv_out = jnp.dot(tap_rows.reshape(-1, 3 * channels), convolution_kernel.reshape(3 * channels, inner_width), preferred_element_type=jnp.float32)
    inner_pre = conv_out.reshape(tap_rows.shape[:3] + (inner_width,)) * scale_two + shift_two
    inner_val, inner_slope = gelu_pair(inner_pre)
    inner_act = inner_val.astype(jnp.bfloat16)
    grad_inner = jnp.dot(grad_top.reshape(-1, channels), out_w.T, preferred_element_type=jnp.float32).reshape(inner_pre.shape)
    grad_conv = (grad_inner * inner_slope * scale_two).astype(jnp.bfloat16)
    grad_pad = jnp.pad(grad_conv, ((0, 0), (0, 0), (dilation_rate, dilation_rate), (0, 0)))
    back_taps = jnp.concatenate([grad_pad[:, :, (2 - tap_number) * dilation_rate: (2 - tap_number) * dilation_rate + LENGTH] for tap_number in range(3)], axis=3)
    back_weight = jnp.transpose(convolution_kernel, (0, 2, 1)).reshape(3 * inner_width, channels)
    grad_hidden = jnp.dot(back_taps.reshape(-1, 3 * inner_width), back_weight, preferred_element_type=jnp.float32).reshape(block_in.shape)
    grad_block = (grad_top.astype(jnp.float32) + grad_hidden * act_slope * scale_one).astype(jnp.bfloat16)
    return tap_rows, inner_act, grad_conv, grad_block


def block_partials(tap_rows, inner_act, grad_conv, grad_top):
    def one_block(block_num):
        start = (block_num * P_DEV).astype(jnp.int32)
        taps_blk = lax.dynamic_slice_in_dim(tap_rows, start, P_DEV, 2).astype(jnp.float32)
        conv_blk = lax.dynamic_slice_in_dim(grad_conv, start, P_DEV, 2).astype(jnp.float32)
        act_blk = lax.dynamic_slice_in_dim(inner_act, start, P_DEV, 2).astype(jnp.float32)
        top_blk = lax.dynamic_slice_in_dim(grad_top, start, P_DEV, 2).astype(jnp.float32)
        conv_part = jnp.sum(round_trip(jnp.einsum('mwpa,mwpi->wai', taps_blk, conv_blk)), axis=0)
        out_part = jnp.sum(round_trip(jnp.einsum('mwpi,mwpc->wic', act_blk, top_blk)), axis=0)
        return conv_part, out_part

    conv_parts, out_parts = lax.map(one_block, jnp.arange(N_SEQ, dtype=jnp.int32))
    return jnp.sum(conv_parts, axis=0), jnp.sum(out_parts, axis=0)


def reference(section_inputs, cotangent, conv_weight, out_weight, norm_scale, norm_shift, inner_scale, inner_shift):
    grad_list = [None] * SECTIONS
    conv_list = [None] * SECTIONS
    out_list = [None] * SECTIONS
    grad_top = cotangent
    factor = 1.0 / float(MICRO * WINDOWS)
    for section_total in range(SECTIONS - 1, -1, -1):
        dilation_rate = BASE_DILATION * (1 + section_total % 2)
        tap_rows, inner_act, grad_conv, grad_block = section_backward(section_inputs[section_total], grad_top, conv_weight[section_total], out_weight[section_total], norm_scale[section_total], norm_shift[section_total], inner_scale[section_total], inner_shift[section_total], dilation_rate)
        conv_sum, out_sum = block_partials(tap_rows, inner_act, grad_conv, grad_top)
        conv_list[section_total] = (conv_sum * factor).reshape(3, C, I)
        out_list[section_total] = out_sum * factor
        grad_list[section_total] = grad_block
        grad_top = grad_block
    return jnp.stack(grad_list), jnp.stack(conv_list), jnp.stack(out_list)
```

```python
import functools

import jax
import jax.numpy as jnp
from jax import lax
from jax.experimental import pallas as pl
from jax.experimental.pallas import tpu as pltpu
from jax.sharding import PartitionSpec as P

BASE_DILATION = 32
MARGIN = 2 * BASE_DILATION
GELU = 0.7978845608028654
CUBIC = 0.044715
MESH = pl.DeviceIdType.MESH
F32 = jnp.float32
BF16 = jnp.bfloat16
NT = (((1,), (1,)), ((), ()))
TN = (((0,), (0,)), ((), ()))


def gelu_pair(z):
    square = z * z
    t = jnp.tanh(z * (GELU + (GELU * CUBIC) * square))
    half = 0.5 + 0.5 * t
    value = z * half
    slope = half + (0.5 * z) * (1.0 - t * t) * (GELU + (3.0 * GELU * CUBIC) * square)
    return value, slope


def y_offsets(ny):
    offsets = [0]
    for dist in range(1, ny // 2 + 1):
        offsets = ([dist] if 2 * dist == ny else [dist, -dist]) + offsets
    return offsets


def kernel(
    sizes,
    x_ref,
    cot_ref,
    cw_ref,
    ow_ref,
    ns_ref,
    nb_ref,
    is_ref,
    ib_ref,
    gin_ref,
    gconv_ref,
    gout_ref,
    hid,
    gcv,
    slope_one,
    slope_two,
    inner,
    act,
    gtop,
    acc,
    part,
    core_in,
    chip,
    xa,
    xb,
    xc,
    row,
    yin,
    col,
    zin,
    final,
    hid_send,
    hid_recv,
    gcv_send,
    gcv_recv,
    sec_send,
    sec_recv,
    core_send,
    core_recv,
    x_send,
    x_recv,
    y_send,
    y_recv,
    z_send,
    z_recv,
    all_send,
    all_recv,
):
    nx, ny, sections = sizes
    micros, rows, channels = x_ref.shape
    width = cw_ref.shape[2]
    block = channels // (2 * ny)
    half_c = channels // 2
    dp = lax.axis_index("dp")
    sec = lax.axis_index("section")
    seq = lax.axis_index("seq")
    x, core = dp // 2, dp % 2
    zh, y = seq // ny, seq % ny
    seqs = 2 * ny
    own = slice(MARGIN, MARGIN + rows)
    parity = sec % 2
    dil = BASE_DILATION * (1 + parity)
    has_prev, has_next = seq > 0, seq < seqs - 1
    is_top = sec == sections - 1

    def device(dp_at=dp, sec_at=sec, seq_at=seq):
        return (dp_at, sec_at, seq_at)

    def remote(src, dst, send, recv, to):
        return pltpu.make_async_remote_copy(
            src_ref=src,
            dst_ref=dst,
            send_sem=send,
            recv_sem=recv,
            device_id=to,
            device_id_type=MESH,
        )

    barrier = pltpu.get_barrier_semaphore()

    def greet(to):
        pl.semaphore_signal(barrier, inc=1, device_id=to, device_id_type=MESH)

    def when_prev(body):
        pl.when(has_prev)(body)

    def when_next(body):
        pl.when(has_next)(body)

    for step in range(1, 2 * nx):
        greet(device(dp_at=lax.rem(dp + step, 2 * nx)))
    for step in range(1, ny):
        greet(device(seq_at=zh * ny + lax.rem(y + step, ny)))
    greet(device(seq_at=(1 - zh) * ny + y))
    crosses_up = jnp.logical_and(zh == 0, y == ny - 1)
    crosses_down = jnp.logical_and(zh == 1, y == 0)
    pl.when(crosses_up)(lambda: greet(device(seq_at=seq + 1)))
    pl.when(crosses_down)(lambda: greet(device(seq_at=seq - 1)))
    pl.when(sec > 0)(lambda: greet(device(sec_at=sec - 1)))
    pl.when(sec < sections - 1)(lambda: greet(device(sec_at=sec + 1)))
    expected = (
        2 * nx - 1 + ny - 1 + 1
        + jnp.where(crosses_up, 1, 0)
        + jnp.where(crosses_down, 1, 0)
        + jnp.where(sec > 0, 1, 0)
        + jnp.where(sec < sections - 1, 1, 0)
    )
    pl.semaphore_wait(barrier, expected)

    def halo(buffer, m, send, recv, step):
        for par in range(2):
            d = BASE_DILATION * (1 + par)

            @pl.when(parity == par)
            def _():
                def up():
                    return remote(
                        buffer.at[m, pl.ds(MARGIN + rows - d, d)],
                        buffer.at[m, pl.ds(MARGIN - d, d)],
                        send.at[m, 0],
                        recv.at[m, 0],
                        device(seq_at=lax.rem(seq + 1, seqs)),
                    )

                def down():
                    return remote(
                        buffer.at[m, pl.ds(MARGIN, d)],
                        buffer.at[m, pl.ds(MARGIN + rows, d)],
                        send.at[m, 1],
                        recv.at[m, 1],
                        device(seq_at=lax.rem(seq + seqs - 1, seqs)),
                    )

                if step == "start":
                    when_next(lambda: up().start())
                    when_prev(lambda: down().start())
                elif step == "recv":
                    when_prev(lambda: up().wait_recv())
                    when_next(lambda: down().wait_recv())
                else:
                    when_next(lambda: up().wait_send())
                    when_prev(lambda: down().wait_send())

    def clear_edges():
        for buffer in (hid, gcv):
            zero = jnp.zeros((micros, MARGIN, buffer.shape[2]), BF16)

            @pl.when(seq == 0)
            def _():
                buffer[:, :MARGIN] = zero

            @pl.when(seq == seqs - 1)
            def _():
                buffer[:, MARGIN + rows :] = zero

    clear_edges()
    tile = 16

    for m in range(micros):

        def activate(i, carry):
            at = pl.multiple_of(i * tile, tile)
            pre = x_ref[m, pl.ds(at, tile), :].astype(F32) * ns_ref[...] + nb_ref[...]
            value, slope = gelu_pair(pre)
            hid[m, pl.ds(MARGIN + at, tile), :] = value.astype(BF16)
            slope_one[m, pl.ds(at, tile), :] = slope * ns_ref[...]
            return carry

        lax.fori_loop(0, rows // tile, activate, 0)
        halo(hid, m, hid_send, hid_recv, "start")

    @pl.when(is_top)
    def _():
        gtop[...] = cot_ref[...]

    def tap_start(k, sign):
        return pl.multiple_of(MARGIN + sign * (k - 1) * dil, BASE_DILATION)

    for m in range(micros):
        halo(hid, m, hid_send, hid_recv, "recv")
        total = None
        for k in range(3):
            term = jnp.dot(
                hid[m, pl.ds(tap_start(k, 1), rows), :], cw_ref[k], preferred_element_type=F32
            )
            total = term if total is None else total + term
        inner[...] = total

        def activate_inner(i, carry):
            at = pl.multiple_of(i * tile, tile)
            pre = inner[pl.ds(at, tile), :] * is_ref[...] + ib_ref[...]
            value, slope = gelu_pair(pre)
            act[m, pl.ds(at, tile), :] = value.astype(BF16)
            slope_two[m, pl.ds(at, tile), :] = slope * is_ref[...]
            return carry

        lax.fori_loop(0, rows // tile, activate_inner, 0)

    pieces = 3
    piece = channels // pieces

    def handed(m, n):
        cut = pl.ds(n * piece, piece)
        return remote(
            gin_ref.at[m, :, cut],
            gtop.at[m, :, cut],
            sec_send.at[m, n],
            sec_recv.at[m, n],
            device(sec_at=lax.rem(sec + sections - 1, sections)),
        )

    def input_grad(m):
        halo(gcv, m, gcv_send, gcv_recv, "recv")
        for n in range(pieces):
            cut = slice(n * piece, (n + 1) * piece)
            total = None
            for k in range(3):
                term = lax.dot_general(
                    gcv[m, pl.ds(tap_start(k, -1), rows), :],
                    cw_ref[k, cut, :],
                    NT,
                    preferred_element_type=F32,
                )
                total = term if total is None else total + term
            gin_ref[m, :, cut] = (
                gtop[m, :, cut].astype(F32) + total * slope_one[m, :, cut]
            ).astype(BF16)
            pl.when(sec > 0)(lambda: handed(m, n).start())

    def weight_grad(m, side):
        cut = pl.ds(pl.multiple_of(side * half_c, 128), half_c)
        for k in range(4):
            if k < 3:
                lhs = hid[m, pl.ds(tap_start(k, 1), rows), cut]
                rhs = gcv[m, own, :]
            else:
                lhs = gtop[m, :, cut]
                rhs = act[m]
            term = lax.dot_general(lhs, rhs, TN, preferred_element_type=F32)
            if m > 0:
                term = term + acc[side, k]
            if m < micros - 1:
                acc[side, k] = term
            else:
                part[side, :, k] = term.reshape(ny, block, width).astype(BF16)

    offsets = y_offsets(ny)
    chunk_y = [lax.rem(y + off + ny, ny) for off in offsets]
    chunks = len(offsets)

    def core_copy(j):
        return remote(
            part.at[1 - core, chunk_y[j]],
            core_in.at[j],
            core_send.at[j],
            core_recv.at[j],
            device(dp_at=dp + 1 - 2 * core),
        )

    for m in range(micros):

        @pl.when(jnp.logical_not(is_top))
        def _():
            for n in range(pieces):
                handed(m, n).wait_recv()

        grad_inner = lax.dot_general(gtop[m], ow_ref[...], NT, preferred_element_type=F32)
        gcv[m, own, :] = (grad_inner * slope_two[m]).astype(BF16)
        halo(gcv, m, gcv_send, gcv_recv, "start")
        weight_grad(m, 1 - core)
        if m == micros - 1:
            for j in range(chunks):
                core_copy(j).start()
        weight_grad(m, core)
        if m < micros - 1:
            input_grad(m)
        else:
            pl.when(sec > 0)(lambda: input_grad(m))

    def x_device(step):
        return device(dp_at=lax.rem(x + step + nx, nx) * 2 + core)

    def x_sign(j):
        return 1 if j % 2 == 0 else -1

    def x_at(step):
        return lax.rem(x + step + nx, nx)

    def x_far(j):
        sign = x_sign(j)
        return remote(
            chip.at[j, x_at(2)], xa.at[j], x_send.at[j, 0], x_recv.at[j, 0], x_device(sign)
        )

    def x_back(j):
        sign = x_sign(j)
        return remote(
            chip.at[j, x_at(-sign)], xb.at[j], x_send.at[j, 1], x_recv.at[j, 1], x_device(-sign)
        )

    def x_ahead(j):
        sign = x_sign(j)
        return remote(
            chip.at[j, x_at(sign)], xc.at[j], x_send.at[j, 2], x_recv.at[j, 2], x_device(sign)
        )

    def y_copy(j):
        return remote(
            row.at[j], yin.at[j], y_send.at[j], y_recv.at[j], device(seq_at=zh * ny + chunk_y[j])
        )

    def stage_core(j):
        core_copy(j).wait_recv()
        chip[j] = (part[core, chunk_y[j]].astype(F32) + core_in[j].astype(F32)).astype(BF16)
        x_far(j).start()
        x_back(j).start()

    def stage_x(j):
        ahead = x_at(x_sign(j))
        x_far(j).wait_recv()
        chip[j, ahead] = (chip[j, ahead].astype(F32) + xa[j].astype(F32)).astype(BF16)
        x_ahead(j).start()

    def stage_y(j):
        x_back(j).wait_recv()
        x_ahead(j).wait_recv()
        total = chip[j, x].astype(F32) + xb[j].astype(F32) + xc[j].astype(F32)
        row[j] = total.astype(BF16)
        if offsets[j] != 0:
            y_copy(j).start()

    lag = 2
    for j in range(chunks + 2 * lag):
        if j < chunks:
            stage_core(j)
        if 0 <= j - lag < chunks:
            stage_x(j - lag)
        if 0 <= j - 2 * lag < chunks:
            stage_y(j - 2 * lag)

    pl.when(sec == 0)(lambda: input_grad(micros - 1))

    total = row[chunks - 1].astype(F32)
    for j in range(chunks - 1):
        y_copy(j).wait_recv()
        total = total + yin[j].astype(F32)
    col[...] = total.astype(BF16)

    def z_copy():
        return remote(col, zin, z_send.at[0], z_recv.at[0], device(seq_at=(1 - zh) * ny + y))

    def spread(step):
        return remote(
            final.at[x],
            final.at[x],
            all_send.at[step],
            all_recv.at[x],
            device(dp_at=lax.rem(dp + step, 2 * nx)),
        )

    def arrival(k):
        return remote(final.at[k], final.at[k], all_send.at[0], all_recv.at[k], device())

    keeps = core == zh
    order = sorted(range(1, 2 * nx), key=lambda s: -min(s, 2 * nx - s))

    @pl.when(jnp.logical_not(keeps))
    def _():
        z_copy().start()

    @pl.when(keeps)
    def _():
        z_copy().wait_recv()
        final[x] = (col[...].astype(F32) + zin[...].astype(F32)).astype(BF16)
        for step in order:
            spread(step).start()

    for k in range(4):
        pl.when(jnp.logical_or(jnp.logical_not(keeps), x != k))(lambda: arrival(k).wait_recv())

    factor = 1.0 / float(micros * 2 * nx)
    for k in range(3):
        gconv_ref[k] = final[k].astype(F32) * factor
    gout_ref[...] = final[3].astype(F32) * factor

    for m in range(micros):
        halo(hid, m, hid_send, hid_recv, "send")
        halo(gcv, m, gcv_send, gcv_recv, "send")

        @pl.when(sec > 0)
        def _():
            for n in range(pieces):
                handed(m, n).wait_send()

    for j in range(chunks):
        core_copy(j).wait_send()
        x_far(j).wait_send()
        x_back(j).wait_send()
        x_ahead(j).wait_send()
        if offsets[j] != 0:
            y_copy(j).wait_send()

    @pl.when(jnp.logical_not(keeps))
    def _():
        z_copy().wait_send()

    @pl.when(keeps)
    def _():
        for step in order:
            spread(step).wait_send()


def on_device(
    sizes,
    section_inputs,
    cotangent,
    conv_weight,
    out_weight,
    norm_scale,
    norm_shift,
    inner_scale,
    inner_shift,
):
    nx, ny, sections = sizes
    inputs = section_inputs[0, :, 0]
    micros, rows, channels = inputs.shape
    width = conv_weight.shape[3]
    block = channels // (2 * ny)
    padded = rows + 2 * MARGIN
    dma = pltpu.SemaphoreType.DMA
    vmem = pl.BlockSpec(memory_space=pltpu.VMEM)
    half_c = channels // 2
    grad_in, grad_conv, grad_out = pl.pallas_call(
        functools.partial(kernel, sizes),
        name="tower_backward",
        out_shape=(
            jax.ShapeDtypeStruct((micros, rows, channels), BF16),
            jax.ShapeDtypeStruct((3, block, width), F32),
            jax.ShapeDtypeStruct((block, width), F32),
        ),
        in_specs=[vmem] * 8,
        out_specs=(vmem,) * 3,
        scratch_shapes=[
            pltpu.VMEM((micros, padded, channels), BF16),
            pltpu.VMEM((micros, padded, width), BF16),
            pltpu.VMEM((micros, rows, channels), F32),
            pltpu.VMEM((micros, rows, width), F32),
            pltpu.VMEM((rows, width), F32),
            pltpu.VMEM((micros, rows, width), BF16),
            pltpu.VMEM((micros, rows, channels), BF16),
            pltpu.VMEM((2, 4, half_c, width), F32),
            pltpu.VMEM((2, ny, 4, block, width), BF16),
            pltpu.VMEM((ny, 4, block, width), BF16),
            pltpu.VMEM((ny, 4, block, width), BF16),
            pltpu.VMEM((ny, block, width), BF16),
            pltpu.VMEM((ny, block, width), BF16),
            pltpu.VMEM((ny, block, width), BF16),
            pltpu.VMEM((ny, block, width), BF16),
            pltpu.VMEM((ny, block, width), BF16),
            pltpu.VMEM((block, width), BF16),
            pltpu.VMEM((block, width), BF16),
            pltpu.VMEM((4, block, width), BF16),
            dma((micros, 2)),
            dma((micros, 2)),
            dma((micros, 2)),
            dma((micros, 2)),
            dma((micros, 3)),
            dma((micros, 3)),
            dma((ny,)),
            dma((ny,)),
            dma((ny, 3)),
            dma((ny, 3)),
            dma((ny,)),
            dma((ny,)),
            dma((1,)),
            dma((1,)),
            dma((2 * nx,)),
            dma((4,)),
        ],
        compiler_params=pltpu.CompilerParams(
            collective_id=0, has_side_effects=True, vmem_limit_bytes=56 * 1024 * 1024
        ),
    )(
        inputs,
        cotangent[:, 0],
        conv_weight[0],
        out_weight[0],
        norm_scale,
        norm_shift,
        inner_scale,
        inner_shift,
    )
    return (
        grad_in.reshape(section_inputs.shape),
        grad_conv[None],
        grad_out.T[None],
    )


def solution(mesh):
    sizes = (mesh.shape["dp"] // 2, mesh.shape["seq"] // 2, mesh.shape["section"])
    return jax.shard_map(
        functools.partial(on_device, sizes),
        mesh=mesh,
        in_specs=(
            P("section", None, "dp", "seq", None),
            P(None, "dp", "seq", None),
            P("section", None, None, None),
            P("section", None, None),
            P("section", None),
            P("section", None),
            P("section", None),
            P("section", None),
        ),
        out_specs=(
            P("section", None, "dp", "seq", None),
            P("section", None, "seq", None),
            P("section", None, "seq"),
        ),
        check_vma=False,
    )
```

```python
import functools

import jax
import jax.numpy as jnp
from jax import lax
from jax.experimental import pallas as pl
from jax.experimental.pallas import tpu as pltpu
from jax.sharding import PartitionSpec as P

BASE_DILATION = 32
MARGIN = 2 * BASE_DILATION
GELU = 0.7978845608028654
CUBIC = 0.044715
MESH = pl.DeviceIdType.MESH
F32 = jnp.float32
BF16 = jnp.bfloat16
TN = (((0,), (0,)), ((), ()))


def gelu_pair(z):
    square = z * z
    t = jnp.tanh(z * (GELU + (GELU * CUBIC) * square))
    half = 0.5 + 0.5 * t
    value = z * half
    slope = half + (0.5 * z) * (1.0 - t * t) * (GELU + (3.0 * GELU * CUBIC) * square)
    return value, slope


def kernel(
    sizes,
    x_in,
    cot_in,
    cw_in,
    ow_in,
    ns_in,
    nb_in,
    is_in,
    ib_in,
    gin_ref,
    total_ref,
    x_ref,
    gtop,
    cw_ref,
    ow_ref,
    ns_ref,
    nb_ref,
    is_ref,
    ib_ref,
    cwt,
    owt,
    hid,
    gcv,
    slope_one,
    slope_two,
    inner,
    act,
    lhs,
    rhs,
    acc,
    row,
    yin,
    col,
    zin,
    load_sem,
    hid_send,
    hid_recv,
    gcv_send,
    gcv_recv,
    sec_send,
    sec_recv,
    lhs_send,
    lhs_recv,
    rhs_send,
    rhs_recv,
    y_send,
    y_recv,
    z_send,
    z_recv,
    all_send,
    all_recv,
):
    nx, ny, sections = sizes
    micros, rows, channels = x_ref.shape
    width = cw_ref.shape[2]
    half_c = channels // 2
    block = half_c // ny
    group = 2 * nx
    dp = lax.axis_index("dp")
    sec = lax.axis_index("section")
    seq = lax.axis_index("seq")
    x, core = dp // 2, dp % 2
    zh, y = seq // ny, seq % ny
    seqs = 2 * ny
    own = slice(MARGIN, MARGIN + rows)
    parity = sec % 2
    dil = BASE_DILATION * (1 + parity)
    has_prev, has_next = seq > 0, seq < seqs - 1
    is_top = sec == sections - 1
    not_top = sec < sections - 1
    is_low = sec == 0
    not_low = sec > 0

    def device(dp_at=dp, sec_at=sec, seq_at=seq):
        return (dp_at, sec_at, seq_at)

    def remote(src, dst, send, recv, to):
        return pltpu.make_async_remote_copy(
            src_ref=src,
            dst_ref=dst,
            send_sem=send,
            recv_sem=recv,
            device_id=to,
            device_id_type=MESH,
        )

    barrier = pltpu.get_barrier_semaphore()

    def greet(to):
        pl.semaphore_signal(barrier, inc=1, device_id=to, device_id_type=MESH)

    for step in range(1, group):
        greet(device(dp_at=lax.rem(dp + step, group)))
    for step in range(1, ny):
        greet(device(seq_at=zh * ny + lax.rem(y + step, ny)))
    greet(device(seq_at=(1 - zh) * ny + y))
    crosses_up = jnp.logical_and(zh == 0, y == ny - 1)
    crosses_down = jnp.logical_and(zh == 1, y == 0)
    pl.when(crosses_up)(lambda: greet(device(seq_at=seq + 1)))
    pl.when(crosses_down)(lambda: greet(device(seq_at=seq - 1)))
    pl.when(not_low)(lambda: greet(device(sec_at=sec - 1)))
    pl.when(not_top)(lambda: greet(device(sec_at=sec + 1)))
    expected = (
        group - 1 + ny - 1 + 1
        + jnp.where(crosses_up, 1, 0)
        + jnp.where(crosses_down, 1, 0)
        + jnp.where(not_low, 1, 0)
        + jnp.where(not_top, 1, 0)
    )

    def load(src, dst, i):
        return pltpu.make_async_copy(src, dst, load_sem.at[i])

    small = ((ns_in, ns_ref), (nb_in, nb_ref), (is_in, is_ref), (ib_in, ib_ref))

    def loads_small():
        return [load(src, dst, i) for i, (src, dst) in enumerate(small)]

    def load_x(m):
        return load(x_in.at[m], x_ref.at[m], 4 + m)

    def load_cw():
        return load(cw_in, cw_ref, 7)

    def load_ow():
        return load(ow_in, ow_ref, 8)

    def load_cot():
        return load(cot_in, gtop, 9)

    for copy in loads_small():
        copy.start()
    for m in range(micros):
        load_x(m).start()
    load_cw().start()
    load_ow().start()
    pl.when(is_top)(lambda: load_cot().start())

    def halo(buffer, m, send, recv, step):
        for par in range(2):
            d = BASE_DILATION * (1 + par)

            @pl.when(parity == par)
            def _():
                def up():
                    return remote(
                        buffer.at[m, pl.ds(MARGIN + rows - d, d)],
                        buffer.at[m, pl.ds(MARGIN - d, d)],
                        send.at[m, 0],
                        recv.at[m, 0],
                        device(seq_at=lax.rem(seq + 1, seqs)),
                    )

                def down():
                    return remote(
                        buffer.at[m, pl.ds(MARGIN, d)],
                        buffer.at[m, pl.ds(MARGIN + rows, d)],
                        send.at[m, 1],
                        recv.at[m, 1],
                        device(seq_at=lax.rem(seq + seqs - 1, seqs)),
                    )

                if step == "start":
                    pl.when(has_next)(lambda: up().start())
                    pl.when(has_prev)(lambda: down().start())
                elif step == "recv":
                    pl.when(has_prev)(lambda: up().wait_recv())
                    pl.when(has_next)(lambda: down().wait_recv())
                else:
                    pl.when(has_next)(lambda: up().wait_send())
                    pl.when(has_prev)(lambda: down().wait_send())

    for buffer in (hid, gcv):
        zero = jnp.zeros((micros, MARGIN, buffer.shape[2]), BF16)

        @pl.when(seq == 0)
        def _():
            buffer[:, :MARGIN] = zero

        @pl.when(seq == seqs - 1)
        def _():
            buffer[:, MARGIN + rows :] = zero

    tile = 16
    for copy in loads_small():
        copy.wait()

    for m in range(micros):
        load_x(m).wait()

        def activate(i, carry):
            at = pl.multiple_of(i * tile, tile)
            pre = x_ref[m, pl.ds(at, tile), :].astype(F32) * ns_ref[...] + nb_ref[...]
            value, slope = gelu_pair(pre)
            hid[m, pl.ds(MARGIN + at, tile), :] = value.astype(BF16)
            slope_one[m, pl.ds(at, tile), :] = slope * ns_ref[...]
            return carry

        lax.fori_loop(0, rows // tile, activate, 0)
        if m == 0:
            pl.semaphore_wait(barrier, expected)
        halo(hid, m, hid_send, hid_recv, "start")

    load_ow().wait()
    owt[...] = ow_ref[...].T
    load_cw().wait()
    for k in range(3):
        cwt[k] = cw_ref[k].T
    pl.when(is_top)(lambda: load_cot().wait())

    def tap_start(k, sign):
        return pl.multiple_of(MARGIN + sign * (k - 1) * dil, BASE_DILATION)

    def inner_forward(m):
        halo(hid, m, hid_send, hid_recv, "recv")
        total = None
        for k in range(3):
            term = jnp.dot(
                hid[m, pl.ds(tap_start(k, 1), rows), :], cw_ref[k], preferred_element_type=F32
            )
            total = term if total is None else total + term
        inner[...] = total

        def activate_inner(i, carry):
            at = pl.multiple_of(i * tile, tile)
            pre = inner[pl.ds(at, tile), :] * is_ref[...] + ib_ref[...]
            value, slope = gelu_pair(pre)
            act[m, pl.ds(at, tile), :] = value.astype(BF16)
            slope_two[m, pl.ds(at, tile), :] = slope * is_ref[...]
            return carry

        lax.fori_loop(0, rows // tile, activate_inner, 0)

    pieces = 3
    piece = channels // pieces

    def handed(m, n):
        cut = pl.ds(n * piece, piece)
        return remote(
            gin_ref.at[m, :, cut],
            gtop.at[m, :, cut],
            sec_send.at[m, n],
            sec_recv.at[m, n],
            device(sec_at=lax.rem(sec + sections - 1, sections)),
        )

    def input_grad(m, send):
        halo(gcv, m, gcv_send, gcv_recv, "recv")
        for n in range(pieces):
            cut = slice(n * piece, (n + 1) * piece)
            total = None
            for k in range(3):
                term = jnp.dot(
                    gcv[m, pl.ds(tap_start(k, -1), rows), :],
                    cwt[k, :, cut],
                    preferred_element_type=F32,
                )
                total = term if total is None else total + term
            gin_ref[m, :, cut] = (
                gtop[m, :, cut].astype(F32) + total * slope_one[m, :, cut]
            ).astype(BF16)
            if send:
                handed(m, n).start()

    steps = sorted(range(1, group), key=lambda t: -min(t, group - t))

    def peer(t):
        to = lax.rem(dp + t, group)
        return to, to // 2, lax.rem(to, 2)

    def half(c):
        return pl.ds(pl.multiple_of(c * half_c, 128), half_c)

    def lhs_tap(m, t):
        to, to_x, to_c = peer(t)
        return remote(
            hid.at[m, pl.ds(tap_start(to_x, 1), rows), half(to_c)],
            lhs.at[m, dp],
            lhs_send.at[m, t],
            lhs_recv.at[m, dp],
            device(dp_at=to),
        )

    def lhs_top(m, t):
        to, _, to_c = peer(t)
        return remote(
            gtop.at[m, :, half(to_c)],
            lhs.at[m, dp],
            lhs_send.at[m, t],
            lhs_recv.at[m, dp],
            device(dp_at=to),
        )

    def rhs_conv(m, t):
        to, _, _ = peer(t)
        return remote(
            gcv.at[m, pl.ds(MARGIN, rows)],
            rhs.at[m, dp],
            rhs_send.at[m, t],
            rhs_recv.at[m, dp],
            device(dp_at=to),
        )

    def rhs_act(m, t):
        to, _, _ = peer(t)
        return remote(
            act.at[m],
            rhs.at[m, dp],
            rhs_send.at[m, t],
            rhs_recv.at[m, dp],
            device(dp_at=to),
        )

    def exchange_early(m):
        for t in steps:
            _, to_x, _ = peer(t)
            pl.when(to_x < 3)(lambda: lhs_tap(m, t).start())
            pl.when(to_x == 3)(lambda: rhs_act(m, t).start())

    def exchange_late(m):
        for t in steps:
            _, to_x, _ = peer(t)
            pl.when(to_x < 3)(lambda: rhs_conv(m, t).start())
            pl.when(to_x == 3)(lambda: lhs_top(m, t).start())

    def weight_grad(m):
        @pl.when(x < 3)
        def _():
            lhs[m, dp] = hid[m, pl.ds(tap_start(x, 1), rows), half(core)]
            rhs[m, dp] = gcv[m, own, :]

        @pl.when(x == 3)
        def _():
            lhs[m, dp] = gtop[m, :, half(core)]
            rhs[m, dp] = act[m]

        for t in steps:
            source = lax.rem(dp + t, group)
            arrival = [
                remote(buffer.at[m, source], buffer.at[m, source], send.at[m, t], recv.at[m, source], device())
                for buffer, send, recv in ((lhs, lhs_send, lhs_recv), (rhs, rhs_send, rhs_recv))
            ]
            for copy in arrival:
                copy.wait_recv()
        term = lax.dot_general(
            lhs[m].reshape(group * rows, half_c),
            rhs[m].reshape(group * rows, width),
            TN,
            preferred_element_type=F32,
        )
        if m > 0:
            term = term + acc[...]
        if m < micros - 1:
            acc[...] = term
        else:
            row[...] = term.reshape(ny, block, width).astype(BF16)

    @pl.when(not_top)
    def _():
        for m in range(micros):
            inner_forward(m)
            exchange_early(m)

    for m in range(micros):

        @pl.when(is_top)
        def _():
            inner_forward(m)

        @pl.when(not_top)
        def _():
            for n in range(pieces):
                handed(m, n).wait_recv()

        grad_inner = jnp.dot(gtop[m], owt[...], preferred_element_type=F32)
        gcv[m, own, :] = (grad_inner * slope_two[m]).astype(BF16)
        halo(gcv, m, gcv_send, gcv_recv, "start")
        pl.when(is_top)(lambda: exchange_early(m))
        exchange_late(m)
        if m > 0:
            pl.when(not_low)(lambda: input_grad(m - 1, True))
    pl.when(not_low)(lambda: input_grad(micros - 1, True))

    weight_grad(0)

    @pl.when(is_low)
    def _():
        for m in range(micros - 1):
            input_grad(m, False)

    for m in range(1, micros):
        weight_grad(m)

    def y_copy(t):
        to = lax.rem(y + t, ny)
        return remote(
            row.at[to], yin.at[t], y_send.at[t], y_recv.at[t], device(seq_at=zh * ny + to)
        )

    far_first = sorted(range(1, ny), key=lambda t: -min(t, ny - t))
    for t in far_first:
        y_copy(t).start()

    pl.when(is_low)(lambda: input_grad(micros - 1, False))

    total = row[y].astype(F32)
    for t in reversed(far_first):
        y_copy(t).wait_recv()
        total = total + yin[t].astype(F32)
    col[...] = total.astype(BF16)

    def z_copy():
        return remote(col, zin, z_send.at[0], z_recv.at[0], device(seq_at=(1 - zh) * ny + y))

    def spread(t):
        return remote(
            total_ref.at[x],
            total_ref.at[x],
            all_send.at[t],
            all_recv.at[x],
            device(dp_at=lax.rem(dp + t, group)),
        )

    def arrival_of(k):
        return remote(total_ref.at[k], total_ref.at[k], all_send.at[0], all_recv.at[k], device())

    keeps = core == zh

    @pl.when(jnp.logical_not(keeps))
    def _():
        z_copy().start()

    @pl.when(keeps)
    def _():
        z_copy().wait_recv()
        total_ref[x] = (col[...].astype(F32) + zin[...].astype(F32)).astype(BF16)
        for t in steps:
            spread(t).start()

    for k in range(4):
        pl.when(jnp.logical_or(jnp.logical_not(keeps), x != k))(lambda: arrival_of(k).wait_recv())

    for m in range(micros):
        halo(hid, m, hid_send, hid_recv, "send")
        halo(gcv, m, gcv_send, gcv_recv, "send")

        @pl.when(not_low)
        def _():
            for n in range(pieces):
                handed(m, n).wait_send()

        for t in steps:
            lhs_top(m, t).wait_send()
            rhs_conv(m, t).wait_send()

    for t in far_first:
        y_copy(t).wait_send()

    @pl.when(jnp.logical_not(keeps))
    def _():
        z_copy().wait_send()

    @pl.when(keeps)
    def _():
        for t in steps:
            spread(t).wait_send()


def finish(factor, gin_in, total_in, gin_ref, gconv_ref, gout_ref):
    gin_ref[...] = gin_in[...]
    gconv_ref[...] = total_in[:3].astype(F32) * factor
    gout_ref[...] = total_in[3].astype(F32) * factor


def on_device(
    sizes,
    section_inputs,
    cotangent,
    conv_weight,
    out_weight,
    norm_scale,
    norm_shift,
    inner_scale,
    inner_shift,
):
    nx, ny, sections = sizes
    inputs = section_inputs[0, :, 0]
    micros, rows, channels = inputs.shape
    width = conv_weight.shape[3]
    half_c = channels // 2
    block = half_c // ny
    group = 2 * nx
    padded = rows + 2 * MARGIN
    dma = pltpu.SemaphoreType.DMA
    vmem = pl.BlockSpec(memory_space=pltpu.VMEM)
    anywhere = pl.BlockSpec(memory_space=pl.ANY)
    grad_in, total = pl.pallas_call(
        functools.partial(kernel, sizes),
        name="tower_backward",
        out_shape=(
            jax.ShapeDtypeStruct((micros, rows, channels), BF16),
            jax.ShapeDtypeStruct((4, block, width), BF16),
        ),
        in_specs=[anywhere] * 8,
        out_specs=(vmem, vmem),
        scratch_shapes=[
            pltpu.VMEM((micros, rows, channels), BF16),
            pltpu.VMEM((micros, rows, channels), BF16),
            pltpu.VMEM((3, channels, width), BF16),
            pltpu.VMEM((width, channels), BF16),
            pltpu.VMEM((1, channels), F32),
            pltpu.VMEM((1, channels), F32),
            pltpu.VMEM((1, width), F32),
            pltpu.VMEM((1, width), F32),
            pltpu.VMEM((3, width, channels), BF16),
            pltpu.VMEM((channels, width), BF16),
            pltpu.VMEM((micros, padded, channels), BF16),
            pltpu.VMEM((micros, padded, width), BF16),
            pltpu.VMEM((micros, rows, channels), F32),
            pltpu.VMEM((micros, rows, width), F32),
            pltpu.VMEM((rows, width), F32),
            pltpu.VMEM((micros, rows, width), BF16),
            pltpu.VMEM((micros, group, rows, half_c), BF16),
            pltpu.VMEM((micros, group, rows, width), BF16),
            pltpu.VMEM((half_c, width), F32),
            pltpu.VMEM((ny, block, width), BF16),
            pltpu.VMEM((ny, block, width), BF16),
            pltpu.VMEM((block, width), BF16),
            pltpu.VMEM((block, width), BF16),
            dma((10,)),
            dma((micros, 2)),
            dma((micros, 2)),
            dma((micros, 2)),
            dma((micros, 2)),
            dma((micros, 3)),
            dma((micros, 3)),
            dma((micros, group)),
            dma((micros, group)),
            dma((micros, group)),
            dma((micros, group)),
            dma((ny,)),
            dma((ny,)),
            dma((1,)),
            dma((1,)),
            dma((group,)),
            dma((4,)),
        ],
        compiler_params=pltpu.CompilerParams(
            collective_id=0, has_side_effects=True, vmem_limit_bytes=56 * 1024 * 1024
        ),
    )(
        inputs,
        cotangent[:, 0],
        conv_weight[0],
        out_weight[0],
        norm_scale,
        norm_shift,
        inner_scale,
        inner_shift,
    )
    grad_in, grad_conv, grad_out = pl.pallas_call(
        functools.partial(finish, 1.0 / float(micros * group)),
        name="write_results",
        out_shape=(
            jax.ShapeDtypeStruct((micros, rows, channels), BF16),
            jax.ShapeDtypeStruct((3, block, width), F32),
            jax.ShapeDtypeStruct((block, width), F32),
        ),
        in_specs=[vmem] * 2,
        out_specs=(vmem,) * 3,
    )(grad_in, total)
    return (
        grad_in.reshape(section_inputs.shape),
        grad_conv[None],
        grad_out.T[None],
    )


def solution(mesh):
    sizes = (mesh.shape["dp"] // 2, mesh.shape["seq"] // 2, mesh.shape["section"])
    return jax.shard_map(
        functools.partial(on_device, sizes),
        mesh=mesh,
        in_specs=(
            P("section", None, "dp", "seq", None),
            P(None, "dp", "seq", None),
            P("section", None, None, None),
            P("section", None, None),
            P("section", None),
            P("section", None),
            P("section", None),
            P("section", None),
        ),
        out_specs=(
            P("section", None, "dp", "seq", None),
            P("section", None, "seq", None),
            P("section", None, "seq"),
        ),
        check_vma=False,
    )
```

```python
import functools

import jax
import jax.numpy as jnp
from jax import lax
from jax.experimental import pallas as pl
from jax.experimental.pallas import tpu as pltpu
from jax.sharding import PartitionSpec as P

BASE_DILATION = 32
MARGIN = 2 * BASE_DILATION
GELU = 0.7978845608028654
CUBIC = 0.044715
MESH = pl.DeviceIdType.MESH
F32 = jnp.float32
BF16 = jnp.bfloat16
TN = (((0,), (0,)), ((), ()))


def gelu_pair(z):
    square = z * z
    t = jnp.tanh(z * (GELU + (GELU * CUBIC) * square))
    half = 0.5 + 0.5 * t
    value = z * half
    slope = half + (0.5 * z) * (1.0 - t * t) * (GELU + (3.0 * GELU * CUBIC) * square)
    return value, slope


def kernel(
    sizes,
    x_in,
    cot_in,
    cw_in,
    ow_in,
    ns_in,
    nb_in,
    is_in,
    ib_in,
    gin_ref,
    total_ref,
    x_ref,
    gtop,
    cw_ref,
    ow_ref,
    ns_ref,
    nb_ref,
    is_ref,
    ib_ref,
    cwt,
    owt,
    hid,
    gcv,
    slope_one,
    slope_two,
    inner,
    act,
    lhs,
    rhs,
    acc,
    row,
    yin,
    col,
    zin,
    load_sem,
    hid_send,
    hid_recv,
    gcv_send,
    gcv_recv,
    sec_send,
    sec_recv,
    lhs_send,
    lhs_recv,
    rhs_send,
    rhs_recv,
    y_send,
    y_recv,
    z_send,
    z_recv,
    all_send,
    all_recv,
):
    nx, ny, sections = sizes
    micros, rows, channels = x_ref.shape
    width = cw_ref.shape[2]
    half_c = channels // 2
    block = half_c // ny
    group = 2 * nx
    dp = lax.axis_index("dp")
    sec = lax.axis_index("section")
    seq = lax.axis_index("seq")
    x, core = dp // 2, dp % 2
    zh, y = seq // ny, seq % ny
    seqs = 2 * ny
    own = slice(MARGIN, MARGIN + rows)
    parity = sec % 2
    dil = BASE_DILATION * (1 + parity)
    has_prev, has_next = seq > 0, seq < seqs - 1
    is_top = sec == sections - 1
    not_top = sec < sections - 1
    is_low = sec == 0
    not_low = sec > 0

    def device(dp_at=dp, sec_at=sec, seq_at=seq):
        return (dp_at, sec_at, seq_at)

    def remote(src, dst, send, recv, to):
        return pltpu.make_async_remote_copy(
            src_ref=src,
            dst_ref=dst,
            send_sem=send,
            recv_sem=recv,
            device_id=to,
            device_id_type=MESH,
        )

    barrier = pltpu.get_barrier_semaphore()

    def greet(to):
        pl.semaphore_signal(barrier, inc=1, device_id=to, device_id_type=MESH)

    for step in range(1, group):
        greet(device(dp_at=lax.rem(dp + step, group)))
    for step in range(1, ny):
        greet(device(seq_at=zh * ny + lax.rem(y + step, ny)))
    greet(device(seq_at=(1 - zh) * ny + y))
    crosses_up = jnp.logical_and(zh == 0, y == ny - 1)
    crosses_down = jnp.logical_and(zh == 1, y == 0)
    pl.when(crosses_up)(lambda: greet(device(seq_at=seq + 1)))
    pl.when(crosses_down)(lambda: greet(device(seq_at=seq - 1)))
    pl.when(not_low)(lambda: greet(device(sec_at=sec - 1)))
    pl.when(not_top)(lambda: greet(device(sec_at=sec + 1)))
    expected = (
        group - 1 + ny - 1 + 1
        + jnp.where(crosses_up, 1, 0)
        + jnp.where(crosses_down, 1, 0)
        + jnp.where(not_low, 1, 0)
        + jnp.where(not_top, 1, 0)
    )

    def load(src, dst, i):
        return pltpu.make_async_copy(src, dst, load_sem.at[i])

    small = ((ns_in, ns_ref), (nb_in, nb_ref), (is_in, is_ref), (ib_in, ib_ref))

    def loads_small():
        return [load(src, dst, i) for i, (src, dst) in enumerate(small)]

    def load_x(m):
        return load(x_in.at[m], x_ref.at[m], 4 + m)

    def load_cw():
        return load(cw_in, cw_ref, 7)

    def load_ow():
        return load(ow_in, ow_ref, 8)

    def load_cot():
        return load(cot_in, gtop, 9)

    for copy in loads_small():
        copy.start()
    for m in range(micros):
        load_x(m).start()
    load_cw().start()
    load_ow().start()
    pl.when(is_top)(lambda: load_cot().start())

    def halo(buffer, m, send, recv, step):
        for par in range(2):
            d = BASE_DILATION * (1 + par)

            @pl.when(parity == par)
            def _():
                def up():
                    return remote(
                        buffer.at[m, pl.ds(MARGIN + rows - d, d)],
                        buffer.at[m, pl.ds(MARGIN - d, d)],
                        send.at[m, 0],
                        recv.at[m, 0],
                        device(seq_at=lax.rem(seq + 1, seqs)),
                    )

                def down():
                    return remote(
                        buffer.at[m, pl.ds(MARGIN, d)],
                        buffer.at[m, pl.ds(MARGIN + rows, d)],
                        send.at[m, 1],
                        recv.at[m, 1],
                        device(seq_at=lax.rem(seq + seqs - 1, seqs)),
                    )

                if step == "start":
                    pl.when(has_next)(lambda: up().start())
                    pl.when(has_prev)(lambda: down().start())
                elif step == "recv":
                    pl.when(has_prev)(lambda: up().wait_recv())
                    pl.when(has_next)(lambda: down().wait_recv())
                else:
                    pl.when(has_next)(lambda: up().wait_send())
                    pl.when(has_prev)(lambda: down().wait_send())

    for buffer in (hid, gcv):
        zero = jnp.zeros((micros, MARGIN, buffer.shape[2]), BF16)

        @pl.when(seq == 0)
        def _():
            buffer[:, :MARGIN] = zero

        @pl.when(seq == seqs - 1)
        def _():
            buffer[:, MARGIN + rows :] = zero

    tile = 16
    for copy in loads_small():
        copy.wait()

    for m in range(micros):
        load_x(m).wait()

        def activate(i, carry):
            at = pl.multiple_of(i * tile, tile)
            pre = x_ref[m, pl.ds(at, tile), :].astype(F32) * ns_ref[...] + nb_ref[...]
            value, slope = gelu_pair(pre)
            hid[m, pl.ds(MARGIN + at, tile), :] = value.astype(BF16)
            slope_one[m, pl.ds(at, tile), :] = slope * ns_ref[...]
            return carry

        lax.fori_loop(0, rows // tile, activate, 0)
        if m == 0:
            pl.semaphore_wait(barrier, expected)
        halo(hid, m, hid_send, hid_recv, "start")

    load_ow().wait()
    owt[...] = ow_ref[...].T
    load_cw().wait()
    for k in range(3):
        cwt[k] = cw_ref[k].T
    pl.when(is_top)(lambda: load_cot().wait())

    def tap_start(k, sign):
        return pl.multiple_of(MARGIN + sign * (k - 1) * dil, BASE_DILATION)

    def inner_forward(m):
        halo(hid, m, hid_send, hid_recv, "recv")
        total = None
        for k in range(3):
            term = jnp.dot(
                hid[m, pl.ds(tap_start(k, 1), rows), :], cw_ref[k], preferred_element_type=F32
            )
            total = term if total is None else total + term
        inner[...] = total

        def activate_inner(i, carry):
            at = pl.multiple_of(i * tile, tile)
            pre = inner[pl.ds(at, tile), :] * is_ref[...] + ib_ref[...]
            value, slope = gelu_pair(pre)
            act[m, pl.ds(at, tile), :] = value.astype(BF16)
            slope_two[m, pl.ds(at, tile), :] = slope * is_ref[...]
            return carry

        lax.fori_loop(0, rows // tile, activate_inner, 0)

    pieces = 3
    piece = channels // pieces

    def handed(m, n):
        cut = pl.ds(n * piece, piece)
        return remote(
            gin_ref.at[m, :, cut],
            gtop.at[m, :, cut],
            sec_send.at[m, n],
            sec_recv.at[m, n],
            device(sec_at=lax.rem(sec + sections - 1, sections)),
        )

    def input_grad(m, send):
        halo(gcv, m, gcv_send, gcv_recv, "recv")
        for n in range(pieces):
            cut = slice(n * piece, (n + 1) * piece)
            total = None
            for k in range(3):
                term = jnp.dot(
                    gcv[m, pl.ds(tap_start(k, -1), rows), :],
                    cwt[k, :, cut],
                    preferred_element_type=F32,
                )
                total = term if total is None else total + term
            gin_ref[m, :, cut] = (
                gtop[m, :, cut].astype(F32) + total * slope_one[m, :, cut]
            ).astype(BF16)
            if send:
                handed(m, n).start()

    steps = sorted(range(1, group), key=lambda t: -min(t, group - t))

    def peer(t):
        to = lax.rem(dp + t, group)
        return to, to // 2, lax.rem(to, 2)

    def half(c):
        return pl.ds(pl.multiple_of(c * half_c, 128), half_c)

    def lhs_tap(m, t):
        to, to_x, to_c = peer(t)
        return remote(
            hid.at[m, pl.ds(tap_start(to_x, 1), rows), half(to_c)],
            lhs.at[m, dp],
            lhs_send.at[m, t],
            lhs_recv.at[m, dp],
            device(dp_at=to),
        )

    def lhs_top(m, t):
        to, _, to_c = peer(t)
        return remote(
            gtop.at[m, :, half(to_c)],
            lhs.at[m, dp],
            lhs_send.at[m, t],
            lhs_recv.at[m, dp],
            device(dp_at=to),
        )

    def rhs_conv(m, t):
        to, _, _ = peer(t)
        return remote(
            gcv.at[m, pl.ds(MARGIN, rows)],
            rhs.at[m, dp],
            rhs_send.at[m, t],
            rhs_recv.at[m, dp],
            device(dp_at=to),
        )

    def rhs_act(m, t):
        to, _, _ = peer(t)
        return remote(
            act.at[m],
            rhs.at[m, dp],
            rhs_send.at[m, t],
            rhs_recv.at[m, dp],
            device(dp_at=to),
        )

    def exchange_early(m):
        for t in steps:
            _, to_x, _ = peer(t)
            pl.when(to_x < 3)(lambda: lhs_tap(m, t).start())
            pl.when(to_x == 3)(lambda: rhs_act(m, t).start())

    def exchange_late(m):
        for t in steps:
            _, to_x, _ = peer(t)
            pl.when(to_x < 3)(lambda: rhs_conv(m, t).start())
            pl.when(to_x == 3)(lambda: lhs_top(m, t).start())

    def weight_grad(m):
        @pl.when(x < 3)
        def _():
            lhs[m, dp] = hid[m, pl.ds(tap_start(x, 1), rows), half(core)]
            rhs[m, dp] = gcv[m, own, :]

        @pl.when(x == 3)
        def _():
            lhs[m, dp] = gtop[m, :, half(core)]
            rhs[m, dp] = act[m]

        for t in steps:
            source = lax.rem(dp + t, group)
            arrival = [
                remote(buffer.at[m, source], buffer.at[m, source], send.at[m, t], recv.at[m, source], device())
                for buffer, send, recv in ((lhs, lhs_send, lhs_recv), (rhs, rhs_send, rhs_recv))
            ]
            for copy in arrival:
                copy.wait_recv()
        term = lax.dot_general(
            lhs[m].reshape(group * rows, half_c),
            rhs[m].reshape(group * rows, width),
            TN,
            preferred_element_type=F32,
        )
        if m > 0:
            term = term + acc[...]
        if m < micros - 1:
            acc[...] = term
        else:
            row[...] = term.reshape(ny, block, width).astype(BF16)

    @pl.when(not_top)
    def _():
        for m in range(micros):
            inner_forward(m)
            exchange_early(m)

    for m in range(micros):

        @pl.when(is_top)
        def _():
            inner_forward(m)

        @pl.when(not_top)
        def _():
            for n in range(pieces):
                handed(m, n).wait_recv()

        grad_inner = jnp.dot(gtop[m], owt[...], preferred_element_type=F32)
        gcv[m, own, :] = (grad_inner * slope_two[m]).astype(BF16)
        halo(gcv, m, gcv_send, gcv_recv, "start")
        if m > 0:
            pl.when(not_low)(lambda: input_grad(m - 1, True))
        if m == micros - 1:
            pl.when(not_low)(lambda: input_grad(m, True))
        pl.when(is_top)(lambda: exchange_early(m))
        exchange_late(m)

    weight_grad(0)

    @pl.when(is_low)
    def _():
        for m in range(micros - 1):
            input_grad(m, False)

    for m in range(1, micros):
        weight_grad(m)

    def y_copy(t):
        to = lax.rem(y + t, ny)
        return remote(
            row.at[to], yin.at[t], y_send.at[t], y_recv.at[t], device(seq_at=zh * ny + to)
        )

    far_first = sorted(range(1, ny), key=lambda t: -min(t, ny - t))
    for t in far_first:
        y_copy(t).start()

    pl.when(is_low)(lambda: input_grad(micros - 1, False))

    total = row[y].astype(F32)
    for t in reversed(far_first):
        y_copy(t).wait_recv()
        total = total + yin[t].astype(F32)
    col[...] = total.astype(BF16)

    def z_copy():
        return remote(col, zin, z_send.at[0], z_recv.at[0], device(seq_at=(1 - zh) * ny + y))

    def spread(t):
        return remote(
            total_ref.at[x],
            total_ref.at[x],
            all_send.at[t],
            all_recv.at[x],
            device(dp_at=lax.rem(dp + t, group)),
        )

    def arrival_of(k):
        return remote(total_ref.at[k], total_ref.at[k], all_send.at[0], all_recv.at[k], device())

    keeps = core == zh

    @pl.when(jnp.logical_not(keeps))
    def _():
        z_copy().start()

    @pl.when(keeps)
    def _():
        z_copy().wait_recv()
        total_ref[x] = (col[...].astype(F32) + zin[...].astype(F32)).astype(BF16)
        for t in steps:
            spread(t).start()

    for k in range(4):
        pl.when(jnp.logical_or(jnp.logical_not(keeps), x != k))(lambda: arrival_of(k).wait_recv())

    for m in range(micros):
        halo(hid, m, hid_send, hid_recv, "send")
        halo(gcv, m, gcv_send, gcv_recv, "send")

        @pl.when(not_low)
        def _():
            for n in range(pieces):
                handed(m, n).wait_send()

        for t in steps:
            lhs_top(m, t).wait_send()
            rhs_conv(m, t).wait_send()

    for t in far_first:
        y_copy(t).wait_send()

    @pl.when(jnp.logical_not(keeps))
    def _():
        z_copy().wait_send()

    @pl.when(keeps)
    def _():
        for t in steps:
            spread(t).wait_send()


def finish(factor, gin_in, total_in, gin_ref, gconv_ref, gout_ref):
    gin_ref[...] = gin_in[...]
    gconv_ref[...] = total_in[:3].astype(F32) * factor
    gout_ref[...] = total_in[3].astype(F32) * factor


def on_device(
    sizes,
    section_inputs,
    cotangent,
    conv_weight,
    out_weight,
    norm_scale,
    norm_shift,
    inner_scale,
    inner_shift,
):
    nx, ny, sections = sizes
    inputs = section_inputs[0, :, 0]
    micros, rows, channels = inputs.shape
    width = conv_weight.shape[3]
    half_c = channels // 2
    block = half_c // ny
    group = 2 * nx
    padded = rows + 2 * MARGIN
    dma = pltpu.SemaphoreType.DMA
    vmem = pl.BlockSpec(memory_space=pltpu.VMEM)
    anywhere = pl.BlockSpec(memory_space=pl.ANY)
    grad_in, total = pl.pallas_call(
        functools.partial(kernel, sizes),
        name="tower_backward",
        out_shape=(
            jax.ShapeDtypeStruct((micros, rows, channels), BF16),
            jax.ShapeDtypeStruct((4, block, width), BF16),
        ),
        in_specs=[anywhere] * 8,
        out_specs=(vmem, vmem),
        scratch_shapes=[
            pltpu.VMEM((micros, rows, channels), BF16),
            pltpu.VMEM((micros, rows, channels), BF16),
            pltpu.VMEM((3, channels, width), BF16),
            pltpu.VMEM((width, channels), BF16),
            pltpu.VMEM((1, channels), F32),
            pltpu.VMEM((1, channels), F32),
            pltpu.VMEM((1, width), F32),
            pltpu.VMEM((1, width), F32),
            pltpu.VMEM((3, width, channels), BF16),
            pltpu.VMEM((channels, width), BF16),
            pltpu.VMEM((micros, padded, channels), BF16),
            pltpu.VMEM((micros, padded, width), BF16),
            pltpu.VMEM((micros, rows, channels), F32),
            pltpu.VMEM((micros, rows, width), F32),
            pltpu.VMEM((rows, width), F32),
            pltpu.VMEM((micros, rows, width), BF16),
            pltpu.VMEM((micros, group, rows, half_c), BF16),
            pltpu.VMEM((micros, group, rows, width), BF16),
            pltpu.VMEM((half_c, width), F32),
            pltpu.VMEM((ny, block, width), BF16),
            pltpu.VMEM((ny, block, width), BF16),
            pltpu.VMEM((block, width), BF16),
            pltpu.VMEM((block, width), BF16),
            dma((10,)),
            dma((micros, 2)),
            dma((micros, 2)),
            dma((micros, 2)),
            dma((micros, 2)),
            dma((micros, 3)),
            dma((micros, 3)),
            dma((micros, group)),
            dma((micros, group)),
            dma((micros, group)),
            dma((micros, group)),
            dma((ny,)),
            dma((ny,)),
            dma((1,)),
            dma((1,)),
            dma((group,)),
            dma((4,)),
        ],
        compiler_params=pltpu.CompilerParams(
            collective_id=0, has_side_effects=True, vmem_limit_bytes=56 * 1024 * 1024
        ),
    )(
        inputs,
        cotangent[:, 0],
        conv_weight[0],
        out_weight[0],
        norm_scale,
        norm_shift,
        inner_scale,
        inner_shift,
    )
    grad_in, grad_conv, grad_out = pl.pallas_call(
        functools.partial(finish, 1.0 / float(micros * group)),
        name="write_results",
        out_shape=(
            jax.ShapeDtypeStruct((micros, rows, channels), BF16),
            jax.ShapeDtypeStruct((3, block, width), F32),
            jax.ShapeDtypeStruct((block, width), F32),
        ),
        in_specs=[vmem] * 2,
        out_specs=(vmem,) * 3,
    )(grad_in, total)
    return (
        grad_in.reshape(section_inputs.shape),
        grad_conv[None],
        grad_out.T[None],
    )


def solution(mesh):
    sizes = (mesh.shape["dp"] // 2, mesh.shape["seq"] // 2, mesh.shape["section"])
    return jax.shard_map(
        functools.partial(on_device, sizes),
        mesh=mesh,
        in_specs=(
            P("section", None, "dp", "seq", None),
            P(None, "dp", "seq", None),
            P("section", None, None, None),
            P("section", None, None),
            P("section", None),
            P("section", None),
            P("section", None),
            P("section", None),
        ),
        out_specs=(
            P("section", None, "dp", "seq", None),
            P("section", None, "seq", None),
            P("section", None, "seq"),
        ),
        check_vma=False,
    )
```

```python
import functools

import jax
import jax.numpy as jnp
from jax import lax
from jax.experimental import pallas as pl
from jax.experimental.pallas import tpu as pltpu
from jax.sharding import PartitionSpec as P

BASE_DILATION = 32
MARGIN = 2 * BASE_DILATION
GELU = 0.7978845608028654
CUBIC = 0.044715
MESH = pl.DeviceIdType.MESH
F32 = jnp.float32
BF16 = jnp.bfloat16
TN = (((0,), (0,)), ((), ()))


def gelu_pair(z):
    square = z * z
    t = jnp.tanh(z * (GELU + (GELU * CUBIC) * square))
    half = 0.5 + 0.5 * t
    value = z * half
    slope = half + (0.5 * z) * (1.0 - t * t) * (GELU + (3.0 * GELU * CUBIC) * square)
    return value, slope


def kernel(
    sizes,
    x_in,
    cot_in,
    cw_in,
    ow_in,
    ns_in,
    nb_in,
    is_in,
    ib_in,
    gin_out,
    total_ref,
    gin_ref,
    x_ref,
    gtop,
    cw_ref,
    ow_ref,
    ns_ref,
    nb_ref,
    is_ref,
    ib_ref,
    cwt,
    owt,
    hid,
    gcv,
    slope_one,
    slope_two,
    inner,
    act,
    lhs,
    rhs,
    acc,
    row,
    yin,
    col,
    zin,
    load_sem,
    hid_send,
    hid_recv,
    gcv_send,
    gcv_recv,
    sec_send,
    sec_recv,
    lhs_send,
    lhs_recv,
    rhs_send,
    rhs_recv,
    y_send,
    y_recv,
    z_send,
    z_recv,
    all_send,
    all_recv,
):
    nx, ny, sections = sizes
    micros, rows, channels = x_ref.shape
    width = cw_ref.shape[2]
    half_c = channels // 2
    block = half_c // ny
    group = 2 * nx
    dp = lax.axis_index("dp")
    sec = lax.axis_index("section")
    seq = lax.axis_index("seq")
    x, core = dp // 2, dp % 2
    zh, y = seq // ny, seq % ny
    seqs = 2 * ny
    own = slice(MARGIN, MARGIN + rows)
    parity = sec % 2
    dil = BASE_DILATION * (1 + parity)
    has_prev, has_next = seq > 0, seq < seqs - 1
    is_top = sec == sections - 1
    not_top = sec < sections - 1
    is_low = sec == 0
    not_low = sec > 0

    def device(dp_at=dp, sec_at=sec, seq_at=seq):
        return (dp_at, sec_at, seq_at)

    def remote(src, dst, send, recv, to):
        return pltpu.make_async_remote_copy(
            src_ref=src,
            dst_ref=dst,
            send_sem=send,
            recv_sem=recv,
            device_id=to,
            device_id_type=MESH,
        )

    barrier = pltpu.get_barrier_semaphore()

    def greet(to):
        pl.semaphore_signal(barrier, inc=1, device_id=to, device_id_type=MESH)

    for step in range(1, group):
        greet(device(dp_at=lax.rem(dp + step, group)))
    for step in range(1, ny):
        greet(device(seq_at=zh * ny + lax.rem(y + step, ny)))
    greet(device(seq_at=(1 - zh) * ny + y))
    crosses_up = jnp.logical_and(zh == 0, y == ny - 1)
    crosses_down = jnp.logical_and(zh == 1, y == 0)
    pl.when(crosses_up)(lambda: greet(device(seq_at=seq + 1)))
    pl.when(crosses_down)(lambda: greet(device(seq_at=seq - 1)))
    pl.when(not_low)(lambda: greet(device(sec_at=sec - 1)))
    pl.when(not_top)(lambda: greet(device(sec_at=sec + 1)))
    expected = (
        group - 1 + ny - 1 + 1
        + jnp.where(crosses_up, 1, 0)
        + jnp.where(crosses_down, 1, 0)
        + jnp.where(not_low, 1, 0)
        + jnp.where(not_top, 1, 0)
    )

    def load(src, dst, i):
        return pltpu.make_async_copy(src, dst, load_sem.at[i])

    small = ((ns_in, ns_ref), (nb_in, nb_ref), (is_in, is_ref), (ib_in, ib_ref))

    def loads_small():
        return [load(src, dst, i) for i, (src, dst) in enumerate(small)]

    def load_x(m):
        return load(x_in.at[m], x_ref.at[m], 4 + m)

    def load_cw():
        return load(cw_in, cw_ref, 7)

    def load_ow():
        return load(ow_in, ow_ref, 8)

    def load_cot():
        return load(cot_in, gtop, 9)

    for copy in loads_small():
        copy.start()
    for m in range(micros):
        load_x(m).start()
    load_cw().start()
    load_ow().start()
    pl.when(is_top)(lambda: load_cot().start())

    def halo(buffer, m, send, recv, step):
        for par in range(2):
            d = BASE_DILATION * (1 + par)

            @pl.when(parity == par)
            def _():
                def up():
                    return remote(
                        buffer.at[m, pl.ds(MARGIN + rows - d, d)],
                        buffer.at[m, pl.ds(MARGIN - d, d)],
                        send.at[m, 0],
                        recv.at[m, 0],
                        device(seq_at=lax.rem(seq + 1, seqs)),
                    )

                def down():
                    return remote(
                        buffer.at[m, pl.ds(MARGIN, d)],
                        buffer.at[m, pl.ds(MARGIN + rows, d)],
                        send.at[m, 1],
                        recv.at[m, 1],
                        device(seq_at=lax.rem(seq + seqs - 1, seqs)),
                    )

                if step == "start":
                    pl.when(has_next)(lambda: up().start())
                    pl.when(has_prev)(lambda: down().start())
                elif step == "recv":
                    pl.when(has_prev)(lambda: up().wait_recv())
                    pl.when(has_next)(lambda: down().wait_recv())
                else:
                    pl.when(has_next)(lambda: up().wait_send())
                    pl.when(has_prev)(lambda: down().wait_send())

    for buffer in (hid, gcv):
        zero = jnp.zeros((micros, MARGIN, buffer.shape[2]), BF16)

        @pl.when(seq == 0)
        def _():
            buffer[:, :MARGIN] = zero

        @pl.when(seq == seqs - 1)
        def _():
            buffer[:, MARGIN + rows :] = zero

    tile = 16
    for copy in loads_small():
        copy.wait()

    for m in range(micros):
        load_x(m).wait()

        def activate(i, carry):
            at = pl.multiple_of(i * tile, tile)
            pre = x_ref[m, pl.ds(at, tile), :].astype(F32) * ns_ref[...] + nb_ref[...]
            value, slope = gelu_pair(pre)
            hid[m, pl.ds(MARGIN + at, tile), :] = value.astype(BF16)
            slope_one[m, pl.ds(at, tile), :] = slope * ns_ref[...]
            return carry

        lax.fori_loop(0, rows // tile, activate, 0)
        if m == 0:
            pl.semaphore_wait(barrier, expected)
        halo(hid, m, hid_send, hid_recv, "start")

    load_ow().wait()
    owt[...] = ow_ref[...].T
    load_cw().wait()
    for k in range(3):
        cwt[k] = cw_ref[k].T
    pl.when(is_top)(lambda: load_cot().wait())

    def tap_start(k, sign):
        return pl.multiple_of(MARGIN + sign * (k - 1) * dil, BASE_DILATION)

    def inner_forward(m):
        halo(hid, m, hid_send, hid_recv, "recv")
        total = None
        for k in range(3):
            term = jnp.dot(
                hid[m, pl.ds(tap_start(k, 1), rows), :], cw_ref[k], preferred_element_type=F32
            )
            total = term if total is None else total + term
        inner[...] = total

        def activate_inner(i, carry):
            at = pl.multiple_of(i * tile, tile)
            pre = inner[pl.ds(at, tile), :] * is_ref[...] + ib_ref[...]
            value, slope = gelu_pair(pre)
            act[m, pl.ds(at, tile), :] = value.astype(BF16)
            slope_two[m, pl.ds(at, tile), :] = slope * is_ref[...]
            return carry

        lax.fori_loop(0, rows // tile, activate_inner, 0)

    pieces = 3
    piece = channels // pieces

    def handed(m, n):
        cut = pl.ds(n * piece, piece)
        return remote(
            gin_ref.at[m, :, cut],
            gtop.at[m, :, cut],
            sec_send.at[m, n],
            sec_recv.at[m, n],
            device(sec_at=lax.rem(sec + sections - 1, sections)),
        )

    def input_grad(m, send):
        halo(gcv, m, gcv_send, gcv_recv, "recv")
        for n in range(pieces):
            cut = slice(n * piece, (n + 1) * piece)
            total = None
            for k in range(3):
                term = jnp.dot(
                    gcv[m, pl.ds(tap_start(k, -1), rows), :],
                    cwt[k, :, cut],
                    preferred_element_type=F32,
                )
                total = term if total is None else total + term
            gin_ref[m, :, cut] = (
                gtop[m, :, cut].astype(F32) + total * slope_one[m, :, cut]
            ).astype(BF16)
            if send:
                handed(m, n).start()

    steps = sorted(range(1, group), key=lambda t: -min(t, group - t))

    def peer(t):
        to = lax.rem(dp + t, group)
        return to, to // 2, lax.rem(to, 2)

    def half(c):
        return pl.ds(pl.multiple_of(c * half_c, 128), half_c)

    def lhs_tap(m, t):
        to, to_x, to_c = peer(t)
        return remote(
            hid.at[m, pl.ds(tap_start(to_x, 1), rows), half(to_c)],
            lhs.at[m, dp],
            lhs_send.at[m, t],
            lhs_recv.at[m, dp],
            device(dp_at=to),
        )

    def lhs_top(m, t):
        to, _, to_c = peer(t)
        return remote(
            gtop.at[m, :, half(to_c)],
            lhs.at[m, dp],
            lhs_send.at[m, t],
            lhs_recv.at[m, dp],
            device(dp_at=to),
        )

    def rhs_conv(m, t):
        to, _, _ = peer(t)
        return remote(
            gcv.at[m, pl.ds(MARGIN, rows)],
            rhs.at[m, dp],
            rhs_send.at[m, t],
            rhs_recv.at[m, dp],
            device(dp_at=to),
        )

    def rhs_act(m, t):
        to, _, _ = peer(t)
        return remote(
            act.at[m],
            rhs.at[m, dp],
            rhs_send.at[m, t],
            rhs_recv.at[m, dp],
            device(dp_at=to),
        )

    def exchange_early(m):
        for t in steps:
            _, to_x, _ = peer(t)
            pl.when(to_x < 3)(lambda: lhs_tap(m, t).start())
            pl.when(to_x == 3)(lambda: rhs_act(m, t).start())

    def exchange_late(m):
        for t in steps:
            _, to_x, _ = peer(t)
            pl.when(to_x < 3)(lambda: rhs_conv(m, t).start())
            pl.when(to_x == 3)(lambda: lhs_top(m, t).start())

    def weight_grad(m):
        @pl.when(x < 3)
        def _():
            lhs[m, dp] = hid[m, pl.ds(tap_start(x, 1), rows), half(core)]
            rhs[m, dp] = gcv[m, own, :]

        @pl.when(x == 3)
        def _():
            lhs[m, dp] = gtop[m, :, half(core)]
            rhs[m, dp] = act[m]

        for t in steps:
            source = lax.rem(dp + t, group)
            arrival = [
                remote(buffer.at[m, source], buffer.at[m, source], send.at[m, t], recv.at[m, source], device())
                for buffer, send, recv in ((lhs, lhs_send, lhs_recv), (rhs, rhs_send, rhs_recv))
            ]
            for copy in arrival:
                copy.wait_recv()
        term = lax.dot_general(
            lhs[m].reshape(group * rows, half_c),
            rhs[m].reshape(group * rows, width),
            TN,
            preferred_element_type=F32,
        )
        if m > 0:
            term = term + acc[...]
        if m < micros - 1:
            acc[...] = term
        else:
            row[...] = term.reshape(ny, block, width).astype(BF16)

    @pl.when(not_top)
    def _():
        for m in range(micros):
            inner_forward(m)
            exchange_early(m)

    for m in range(micros):

        @pl.when(is_top)
        def _():
            inner_forward(m)

        @pl.when(not_top)
        def _():
            for n in range(pieces):
                handed(m, n).wait_recv()

        grad_inner = jnp.dot(gtop[m], owt[...], preferred_element_type=F32)
        gcv[m, own, :] = (grad_inner * slope_two[m]).astype(BF16)
        halo(gcv, m, gcv_send, gcv_recv, "start")
        pl.when(is_top)(lambda: exchange_early(m))
        exchange_late(m)
        if m > 0:
            pl.when(not_low)(lambda: input_grad(m - 1, True))
    pl.when(not_low)(lambda: input_grad(micros - 1, True))

    weight_grad(0)

    @pl.when(is_low)
    def _():
        for m in range(micros - 1):
            input_grad(m, False)

    for m in range(1, micros):
        weight_grad(m)

    def y_copy(t):
        to = lax.rem(y + t, ny)
        return remote(
            row.at[to], yin.at[t], y_send.at[t], y_recv.at[t], device(seq_at=zh * ny + to)
        )

    far_first = sorted(range(1, ny), key=lambda t: -min(t, ny - t))
    for t in far_first:
        y_copy(t).start()

    pl.when(is_low)(lambda: input_grad(micros - 1, False))

    def store_gin(m):
        return pltpu.make_async_copy(gin_ref.at[m], gin_out.at[m], load_sem.at[10 + m])

    for m in range(micros):
        store_gin(m).start()

    total = row[y].astype(F32)
    for t in reversed(far_first):
        y_copy(t).wait_recv()
        total = total + yin[t].astype(F32)
    col[...] = total.astype(BF16)

    def z_copy():
        return remote(col, zin, z_send.at[0], z_recv.at[0], device(seq_at=(1 - zh) * ny + y))

    def spread(t):
        return remote(
            total_ref.at[x],
            total_ref.at[x],
            all_send.at[t],
            all_recv.at[x],
            device(dp_at=lax.rem(dp + t, group)),
        )

    def arrival_of(k):
        return remote(total_ref.at[k], total_ref.at[k], all_send.at[0], all_recv.at[k], device())

    keeps = core == zh

    @pl.when(jnp.logical_not(keeps))
    def _():
        z_copy().start()

    @pl.when(keeps)
    def _():
        z_copy().wait_recv()
        total_ref[x] = (col[...].astype(F32) + zin[...].astype(F32)).astype(BF16)
        for t in steps:
            spread(t).start()

    for k in range(4):
        pl.when(jnp.logical_or(jnp.logical_not(keeps), x != k))(lambda: arrival_of(k).wait_recv())

    for m in range(micros):
        halo(hid, m, hid_send, hid_recv, "send")
        halo(gcv, m, gcv_send, gcv_recv, "send")

        @pl.when(not_low)
        def _():
            for n in range(pieces):
                handed(m, n).wait_send()

        for t in steps:
            lhs_top(m, t).wait_send()
            rhs_conv(m, t).wait_send()

    for t in far_first:
        y_copy(t).wait_send()
    for m in range(micros):
        store_gin(m).wait()

    @pl.when(jnp.logical_not(keeps))
    def _():
        z_copy().wait_send()

    @pl.when(keeps)
    def _():
        for t in steps:
            spread(t).wait_send()


def finish(factor, gin_in, total_in, gin_out, gconv_ref, gout_ref, held, sem):
    fetch = pltpu.make_async_copy(gin_in, held, sem.at[0])
    store = pltpu.make_async_copy(held, gin_out, sem.at[1])
    fetch.start()
    gconv_ref[...] = total_in[:3].astype(F32) * factor
    gout_ref[...] = total_in[3].astype(F32) * factor
    fetch.wait()
    store.start()
    store.wait()


def on_device(
    sizes,
    section_inputs,
    cotangent,
    conv_weight,
    out_weight,
    norm_scale,
    norm_shift,
    inner_scale,
    inner_shift,
):
    nx, ny, sections = sizes
    inputs = section_inputs[0, :, 0]
    micros, rows, channels = inputs.shape
    width = conv_weight.shape[3]
    half_c = channels // 2
    block = half_c // ny
    group = 2 * nx
    padded = rows + 2 * MARGIN
    dma = pltpu.SemaphoreType.DMA
    vmem = pl.BlockSpec(memory_space=pltpu.VMEM)
    anywhere = pl.BlockSpec(memory_space=pl.ANY)
    grad_in, total = pl.pallas_call(
        functools.partial(kernel, sizes),
        name="tower_backward",
        out_shape=(
            jax.ShapeDtypeStruct((micros, rows, channels), BF16),
            jax.ShapeDtypeStruct((4, block, width), BF16),
        ),
        in_specs=[anywhere] * 8,
        out_specs=(anywhere, vmem),
        scratch_shapes=[
            pltpu.VMEM((micros, rows, channels), BF16),
            pltpu.VMEM((micros, rows, channels), BF16),
            pltpu.VMEM((micros, rows, channels), BF16),
            pltpu.VMEM((3, channels, width), BF16),
            pltpu.VMEM((width, channels), BF16),
            pltpu.VMEM((1, channels), F32),
            pltpu.VMEM((1, channels), F32),
            pltpu.VMEM((1, width), F32),
            pltpu.VMEM((1, width), F32),
            pltpu.VMEM((3, width, channels), BF16),
            pltpu.VMEM((channels, width), BF16),
            pltpu.VMEM((micros, padded, channels), BF16),
            pltpu.VMEM((micros, padded, width), BF16),
            pltpu.VMEM((micros, rows, channels), F32),
            pltpu.VMEM((micros, rows, width), F32),
            pltpu.VMEM((rows, width), F32),
            pltpu.VMEM((micros, rows, width), BF16),
            pltpu.VMEM((micros, group, rows, half_c), BF16),
            pltpu.VMEM((micros, group, rows, width), BF16),
            pltpu.VMEM((half_c, width), F32),
            pltpu.VMEM((ny, block, width), BF16),
            pltpu.VMEM((ny, block, width), BF16),
            pltpu.VMEM((block, width), BF16),
            pltpu.VMEM((block, width), BF16),
            dma((13,)),
            dma((micros, 2)),
            dma((micros, 2)),
            dma((micros, 2)),
            dma((micros, 2)),
            dma((micros, 3)),
            dma((micros, 3)),
            dma((micros, group)),
            dma((micros, group)),
            dma((micros, group)),
            dma((micros, group)),
            dma((ny,)),
            dma((ny,)),
            dma((1,)),
            dma((1,)),
            dma((group,)),
            dma((4,)),
        ],
        compiler_params=pltpu.CompilerParams(
            collective_id=0, has_side_effects=True, vmem_limit_bytes=56 * 1024 * 1024
        ),
    )(
        inputs,
        cotangent[:, 0],
        conv_weight[0],
        out_weight[0],
        norm_scale,
        norm_shift,
        inner_scale,
        inner_shift,
    )
    grad_in, grad_conv, grad_out = pl.pallas_call(
        functools.partial(finish, 1.0 / float(micros * group)),
        name="write_results",
        out_shape=(
            jax.ShapeDtypeStruct((micros, rows, channels), BF16),
            jax.ShapeDtypeStruct((3, block, width), F32),
            jax.ShapeDtypeStruct((block, width), F32),
        ),
        in_specs=[anywhere, vmem],
        out_specs=(anywhere, vmem, vmem),
        scratch_shapes=[pltpu.VMEM((micros, rows, channels), BF16), dma((2,))],
    )(grad_in, total)
    return (
        grad_in.reshape(section_inputs.shape),
        grad_conv[None],
        grad_out.T[None],
    )


def solution(mesh):
    sizes = (mesh.shape["dp"] // 2, mesh.shape["seq"] // 2, mesh.shape["section"])
    return jax.shard_map(
        functools.partial(on_device, sizes),
        mesh=mesh,
        in_specs=(
            P("section", None, "dp", "seq", None),
            P(None, "dp", "seq", None),
            P("section", None, None, None),
            P("section", None, None),
            P("section", None),
            P("section", None),
            P("section", None),
            P("section", None),
        ),
        out_specs=(
            P("section", None, "dp", "seq", None),
            P("section", None, "seq", None),
            P("section", None, "seq"),
        ),
        check_vma=False,
    )
```

```python
import functools

import jax
import jax.numpy as jnp
from jax import lax
from jax.experimental import pallas as pl
from jax.experimental.pallas import tpu as pltpu
from jax.sharding import PartitionSpec as P

BASE_DILATION = 32
MARGIN = 2 * BASE_DILATION
GELU = 0.7978845608028654
CUBIC = 0.044715
MESH = pl.DeviceIdType.MESH
F32 = jnp.float32
BF16 = jnp.bfloat16
TN = (((0,), (0,)), ((), ()))


def gelu_pair(z):
    square = z * z
    t = jnp.tanh(z * (GELU + (GELU * CUBIC) * square))
    half = 0.5 + 0.5 * t
    value = z * half
    slope = half + (0.5 * z) * (1.0 - t * t) * (GELU + (3.0 * GELU * CUBIC) * square)
    return value, slope


def kernel(
    sizes,
    x_in,
    cot_in,
    cw_in,
    ow_in,
    ns_in,
    nb_in,
    is_in,
    ib_in,
    gin_ref,
    total_ref,
    x_ref,
    gtop,
    cw_ref,
    ow_ref,
    ns_ref,
    nb_ref,
    is_ref,
    ib_ref,
    cwt,
    owt,
    hid,
    gcv,
    slope_one,
    slope_two,
    inner,
    act,
    lhs,
    rhs,
    acc,
    row,
    yin,
    col,
    zin,
    load_sem,
    hid_send,
    hid_recv,
    gcv_send,
    gcv_recv,
    sec_send,
    sec_recv,
    lhs_send,
    lhs_recv,
    rhs_send,
    rhs_recv,
    y_send,
    y_recv,
    z_send,
    z_recv,
    all_send,
    all_recv,
):
    nx, ny, sections = sizes
    micros, rows, channels = x_ref.shape
    width = cw_ref.shape[2]
    half_c = channels // 2
    block = half_c // ny
    group = 2 * nx
    dp = lax.axis_index("dp")
    sec = lax.axis_index("section")
    seq = lax.axis_index("seq")
    x, core = dp // 2, dp % 2
    zh, y = seq // ny, seq % ny
    seqs = 2 * ny
    own = slice(MARGIN, MARGIN + rows)
    parity = sec % 2
    dil = BASE_DILATION * (1 + parity)
    has_prev, has_next = seq > 0, seq < seqs - 1
    is_top = sec == sections - 1
    not_top = sec < sections - 1
    is_low = sec == 0
    not_low = sec > 0

    def device(dp_at=dp, sec_at=sec, seq_at=seq):
        return (dp_at, sec_at, seq_at)

    def remote(src, dst, send, recv, to):
        return pltpu.make_async_remote_copy(
            src_ref=src,
            dst_ref=dst,
            send_sem=send,
            recv_sem=recv,
            device_id=to,
            device_id_type=MESH,
        )

    barrier = pltpu.get_barrier_semaphore()

    def greet(to):
        pl.semaphore_signal(barrier, inc=1, device_id=to, device_id_type=MESH)

    for step in range(1, group):
        greet(device(dp_at=lax.rem(dp + step, group)))
    for step in range(1, ny):
        greet(device(seq_at=zh * ny + lax.rem(y + step, ny)))
    greet(device(seq_at=(1 - zh) * ny + y))
    crosses_up = jnp.logical_and(zh == 0, y == ny - 1)
    crosses_down = jnp.logical_and(zh == 1, y == 0)
    pl.when(crosses_up)(lambda: greet(device(seq_at=seq + 1)))
    pl.when(crosses_down)(lambda: greet(device(seq_at=seq - 1)))
    pl.when(not_low)(lambda: greet(device(sec_at=sec - 1)))
    pl.when(not_top)(lambda: greet(device(sec_at=sec + 1)))
    expected = (
        group - 1 + ny - 1 + 1
        + jnp.where(crosses_up, 1, 0)
        + jnp.where(crosses_down, 1, 0)
        + jnp.where(not_low, 1, 0)
        + jnp.where(not_top, 1, 0)
    )

    def load(src, dst, i):
        return pltpu.make_async_copy(src, dst, load_sem.at[i])

    small = ((ns_in, ns_ref), (nb_in, nb_ref), (is_in, is_ref), (ib_in, ib_ref))

    def loads_small():
        return [load(src, dst, i) for i, (src, dst) in enumerate(small)]

    def load_x(m):
        return load(x_in.at[m], x_ref.at[m], 4 + m)

    def load_cw():
        return load(cw_in, cw_ref, 7)

    def load_ow():
        return load(ow_in, ow_ref, 8)

    def load_cot():
        return load(cot_in, gtop, 9)

    for copy in loads_small():
        copy.start()
    for m in range(micros):
        load_x(m).start()
    load_cw().start()
    load_ow().start()
    pl.when(is_top)(lambda: load_cot().start())

    def halo(buffer, m, send, recv, step):
        for par in range(2):
            d = BASE_DILATION * (1 + par)

            @pl.when(parity == par)
            def _():
                def up():
                    return remote(
                        buffer.at[m, pl.ds(MARGIN + rows - d, d)],
                        buffer.at[m, pl.ds(MARGIN - d, d)],
                        send.at[m, 0],
                        recv.at[m, 0],
                        device(seq_at=lax.rem(seq + 1, seqs)),
                    )

                def down():
                    return remote(
                        buffer.at[m, pl.ds(MARGIN, d)],
                        buffer.at[m, pl.ds(MARGIN + rows, d)],
                        send.at[m, 1],
                        recv.at[m, 1],
                        device(seq_at=lax.rem(seq + seqs - 1, seqs)),
                    )

                if step == "start":
                    pl.when(has_next)(lambda: up().start())
                    pl.when(has_prev)(lambda: down().start())
                elif step == "recv":
                    pl.when(has_prev)(lambda: up().wait_recv())
                    pl.when(has_next)(lambda: down().wait_recv())
                else:
                    pl.when(has_next)(lambda: up().wait_send())
                    pl.when(has_prev)(lambda: down().wait_send())

    for buffer in (hid, gcv):
        zero = jnp.zeros((micros, MARGIN, buffer.shape[2]), BF16)

        @pl.when(seq == 0)
        def _():
            buffer[:, :MARGIN] = zero

        @pl.when(seq == seqs - 1)
        def _():
            buffer[:, MARGIN + rows :] = zero

    tile = 16
    for copy in loads_small():
        copy.wait()

    for m in range(micros):
        load_x(m).wait()

        def activate(i, carry):
            at = pl.multiple_of(i * tile, tile)
            pre = x_ref[m, pl.ds(at, tile), :].astype(F32) * ns_ref[...] + nb_ref[...]
            value, slope = gelu_pair(pre)
            hid[m, pl.ds(MARGIN + at, tile), :] = value.astype(BF16)
            slope_one[m, pl.ds(at, tile), :] = slope * ns_ref[...]
            return carry

        lax.fori_loop(0, rows // tile, activate, 0)
        if m == 0:
            pl.semaphore_wait(barrier, expected)
        halo(hid, m, hid_send, hid_recv, "start")

    load_ow().wait()
    owt[...] = ow_ref[...].T
    load_cw().wait()
    for k in range(3):
        cwt[k] = cw_ref[k].T
    pl.when(is_top)(lambda: load_cot().wait())

    def tap_start(k, sign):
        return pl.multiple_of(MARGIN + sign * (k - 1) * dil, BASE_DILATION)

    def inner_forward(m):
        halo(hid, m, hid_send, hid_recv, "recv")
        total = None
        for k in range(3):
            term = jnp.dot(
                hid[m, pl.ds(tap_start(k, 1), rows), :], cw_ref[k], preferred_element_type=F32
            )
            total = term if total is None else total + term
        inner[...] = total

        def activate_inner(i, carry):
            at = pl.multiple_of(i * tile, tile)
            pre = inner[pl.ds(at, tile), :] * is_ref[...] + ib_ref[...]
            value, slope = gelu_pair(pre)
            act[m, pl.ds(at, tile), :] = value.astype(BF16)
            slope_two[m, pl.ds(at, tile), :] = slope * is_ref[...]
            return carry

        lax.fori_loop(0, rows // tile, activate_inner, 0)

    pieces = 2
    piece = channels // pieces

    def handed(m, n):
        cut = pl.ds(n * piece, piece)
        return remote(
            gin_ref.at[m, :, cut],
            gtop.at[m, :, cut],
            sec_send.at[m, n],
            sec_recv.at[m, n],
            device(sec_at=lax.rem(sec + sections - 1, sections)),
        )

    def input_grad(m, send):
        halo(gcv, m, gcv_send, gcv_recv, "recv")
        for n in range(pieces):
            cut = slice(n * piece, (n + 1) * piece)
            total = None
            for k in range(3):
                term = jnp.dot(
                    gcv[m, pl.ds(tap_start(k, -1), rows), :],
                    cwt[k, :, cut],
                    preferred_element_type=F32,
                )
                total = term if total is None else total + term
            gin_ref[m, :, cut] = (
                gtop[m, :, cut].astype(F32) + total * slope_one[m, :, cut]
            ).astype(BF16)
            if send:
                handed(m, n).start()

    steps = sorted(range(1, group), key=lambda t: -min(t, group - t))

    def peer(t):
        to = lax.rem(dp + t, group)
        return to, to // 2, lax.rem(to, 2)

    def half(c):
        return pl.ds(pl.multiple_of(c * half_c, 128), half_c)

    def lhs_tap(m, t):
        to, to_x, to_c = peer(t)
        return remote(
            hid.at[m, pl.ds(tap_start(to_x, 1), rows), half(to_c)],
            lhs.at[m, dp],
            lhs_send.at[m, t],
            lhs_recv.at[m, dp],
            device(dp_at=to),
        )

    def lhs_top(m, t):
        to, _, to_c = peer(t)
        return remote(
            gtop.at[m, :, half(to_c)],
            lhs.at[m, dp],
            lhs_send.at[m, t],
            lhs_recv.at[m, dp],
            device(dp_at=to),
        )

    def rhs_conv(m, t):
        to, _, _ = peer(t)
        return remote(
            gcv.at[m, pl.ds(MARGIN, rows)],
            rhs.at[m, dp],
            rhs_send.at[m, t],
            rhs_recv.at[m, dp],
            device(dp_at=to),
        )

    def rhs_act(m, t):
        to, _, _ = peer(t)
        return remote(
            act.at[m],
            rhs.at[m, dp],
            rhs_send.at[m, t],
            rhs_recv.at[m, dp],
            device(dp_at=to),
        )

    def exchange_early(m):
        for t in steps:
            _, to_x, _ = peer(t)
            pl.when(to_x < 3)(lambda: lhs_tap(m, t).start())
            pl.when(to_x == 3)(lambda: rhs_act(m, t).start())

    def exchange_late(m):
        for t in steps:
            _, to_x, _ = peer(t)
            pl.when(to_x < 3)(lambda: rhs_conv(m, t).start())
            pl.when(to_x == 3)(lambda: lhs_top(m, t).start())

    def weight_grad(m):
        @pl.when(x < 3)
        def _():
            lhs[m, dp] = hid[m, pl.ds(tap_start(x, 1), rows), half(core)]
            rhs[m, dp] = gcv[m, own, :]

        @pl.when(x == 3)
        def _():
            lhs[m, dp] = gtop[m, :, half(core)]
            rhs[m, dp] = act[m]

        for t in steps:
            source = lax.rem(dp + t, group)
            arrival = [
                remote(buffer.at[m, source], buffer.at[m, source], send.at[m, t], recv.at[m, source], device())
                for buffer, send, recv in ((lhs, lhs_send, lhs_recv), (rhs, rhs_send, rhs_recv))
            ]
            for copy in arrival:
                copy.wait_recv()
        term = lax.dot_general(
            lhs[m].reshape(group * rows, half_c),
            rhs[m].reshape(group * rows, width),
            TN,
            preferred_element_type=F32,
        )
        if m > 0:
            term = term + acc[...]
        if m < micros - 1:
            acc[...] = term
        else:
            row[...] = term.reshape(ny, block, width).astype(BF16)

    @pl.when(not_top)
    def _():
        for m in range(micros):
            inner_forward(m)
            exchange_early(m)

    for m in range(micros):

        @pl.when(is_top)
        def _():
            inner_forward(m)

        @pl.when(not_top)
        def _():
            for n in range(pieces):
                handed(m, n).wait_recv()

        grad_inner = jnp.dot(gtop[m], owt[...], preferred_element_type=F32)
        gcv[m, own, :] = (grad_inner * slope_two[m]).astype(BF16)
        halo(gcv, m, gcv_send, gcv_recv, "start")
        pl.when(is_top)(lambda: exchange_early(m))
        exchange_late(m)
        if m > 0:
            pl.when(not_low)(lambda: input_grad(m - 1, True))
    pl.when(not_low)(lambda: input_grad(micros - 1, True))

    weight_grad(0)

    @pl.when(is_low)
    def _():
        for m in range(micros - 1):
            input_grad(m, False)

    for m in range(1, micros):
        weight_grad(m)

    def y_copy(t):
        to = lax.rem(y + t, ny)
        return remote(
            row.at[to], yin.at[t], y_send.at[t], y_recv.at[t], device(seq_at=zh * ny + to)
        )

    far_first = sorted(range(1, ny), key=lambda t: -min(t, ny - t))
    for t in far_first:
        y_copy(t).start()

    pl.when(is_low)(lambda: input_grad(micros - 1, False))

    total = row[y].astype(F32)
    for t in reversed(far_first):
        y_copy(t).wait_recv()
        total = total + yin[t].astype(F32)
    col[...] = total.astype(BF16)

    def z_copy():
        return remote(col, zin, z_send.at[0], z_recv.at[0], device(seq_at=(1 - zh) * ny + y))

    def spread(t):
        return remote(
            total_ref.at[x],
            total_ref.at[x],
            all_send.at[t],
            all_recv.at[x],
            device(dp_at=lax.rem(dp + t, group)),
        )

    def arrival_of(k):
        return remote(total_ref.at[k], total_ref.at[k], all_send.at[0], all_recv.at[k], device())

    keeps = core == zh

    @pl.when(jnp.logical_not(keeps))
    def _():
        z_copy().start()

    @pl.when(keeps)
    def _():
        z_copy().wait_recv()
        total_ref[x] = (col[...].astype(F32) + zin[...].astype(F32)).astype(BF16)
        for t in steps:
            spread(t).start()

    for k in range(4):
        pl.when(jnp.logical_or(jnp.logical_not(keeps), x != k))(lambda: arrival_of(k).wait_recv())

    for m in range(micros):
        halo(hid, m, hid_send, hid_recv, "send")
        halo(gcv, m, gcv_send, gcv_recv, "send")

        @pl.when(not_low)
        def _():
            for n in range(pieces):
                handed(m, n).wait_send()

        for t in steps:
            lhs_top(m, t).wait_send()
            rhs_conv(m, t).wait_send()

    for t in far_first:
        y_copy(t).wait_send()

    @pl.when(jnp.logical_not(keeps))
    def _():
        z_copy().wait_send()

    @pl.when(keeps)
    def _():
        for t in steps:
            spread(t).wait_send()


def finish(factor, gin_in, total_in, gin_ref, gconv_ref, gout_ref):
    gin_ref[...] = gin_in[...]
    gconv_ref[...] = total_in[:3].astype(F32) * factor
    gout_ref[...] = total_in[3].astype(F32) * factor


def on_device(
    sizes,
    section_inputs,
    cotangent,
    conv_weight,
    out_weight,
    norm_scale,
    norm_shift,
    inner_scale,
    inner_shift,
):
    nx, ny, sections = sizes
    inputs = section_inputs[0, :, 0]
    micros, rows, channels = inputs.shape
    width = conv_weight.shape[3]
    half_c = channels // 2
    block = half_c // ny
    group = 2 * nx
    padded = rows + 2 * MARGIN
    dma = pltpu.SemaphoreType.DMA
    vmem = pl.BlockSpec(memory_space=pltpu.VMEM)
    anywhere = pl.BlockSpec(memory_space=pl.ANY)
    grad_in, total = pl.pallas_call(
        functools.partial(kernel, sizes),
        name="tower_backward",
        out_shape=(
            jax.ShapeDtypeStruct((micros, rows, channels), BF16),
            jax.ShapeDtypeStruct((4, block, width), BF16),
        ),
        in_specs=[anywhere] * 8,
        out_specs=(vmem, vmem),
        scratch_shapes=[
            pltpu.VMEM((micros, rows, channels), BF16),
            pltpu.VMEM((micros, rows, channels), BF16),
            pltpu.VMEM((3, channels, width), BF16),
            pltpu.VMEM((width, channels), BF16),
            pltpu.VMEM((1, channels), F32),
            pltpu.VMEM((1, channels), F32),
            pltpu.VMEM((1, width), F32),
            pltpu.VMEM((1, width), F32),
            pltpu.VMEM((3, width, channels), BF16),
            pltpu.VMEM((channels, width), BF16),
            pltpu.VMEM((micros, padded, channels), BF16),
            pltpu.VMEM((micros, padded, width), BF16),
            pltpu.VMEM((micros, rows, channels), F32),
            pltpu.VMEM((micros, rows, width), F32),
            pltpu.VMEM((rows, width), F32),
            pltpu.VMEM((micros, rows, width), BF16),
            pltpu.VMEM((micros, group, rows, half_c), BF16),
            pltpu.VMEM((micros, group, rows, width), BF16),
            pltpu.VMEM((half_c, width), F32),
            pltpu.VMEM((ny, block, width), BF16),
            pltpu.VMEM((ny, block, width), BF16),
            pltpu.VMEM((block, width), BF16),
            pltpu.VMEM((block, width), BF16),
            dma((10,)),
            dma((micros, 2)),
            dma((micros, 2)),
            dma((micros, 2)),
            dma((micros, 2)),
            dma((micros, 3)),
            dma((micros, 3)),
            dma((micros, group)),
            dma((micros, group)),
            dma((micros, group)),
            dma((micros, group)),
            dma((ny,)),
            dma((ny,)),
            dma((1,)),
            dma((1,)),
            dma((group,)),
            dma((4,)),
        ],
        compiler_params=pltpu.CompilerParams(
            collective_id=0, has_side_effects=True, vmem_limit_bytes=56 * 1024 * 1024
        ),
    )(
        inputs,
        cotangent[:, 0],
        conv_weight[0],
        out_weight[0],
        norm_scale,
        norm_shift,
        inner_scale,
        inner_shift,
    )
    grad_in, grad_conv, grad_out = pl.pallas_call(
        functools.partial(finish, 1.0 / float(micros * group)),
        name="write_results",
        out_shape=(
            jax.ShapeDtypeStruct((micros, rows, channels), BF16),
            jax.ShapeDtypeStruct((3, block, width), F32),
            jax.ShapeDtypeStruct((block, width), F32),
        ),
        in_specs=[vmem] * 2,
        out_specs=(vmem,) * 3,
    )(grad_in, total)
    return (
        grad_in.reshape(section_inputs.shape),
        grad_conv[None],
        grad_out.T[None],
    )


def solution(mesh):
    sizes = (mesh.shape["dp"] // 2, mesh.shape["seq"] // 2, mesh.shape["section"])
    return jax.shard_map(
        functools.partial(on_device, sizes),
        mesh=mesh,
        in_specs=(
            P("section", None, "dp", "seq", None),
            P(None, "dp", "seq", None),
            P("section", None, None, None),
            P("section", None, None),
            P("section", None),
            P("section", None),
            P("section", None),
            P("section", None),
        ),
        out_specs=(
            P("section", None, "dp", "seq", None),
            P("section", None, "seq", None),
            P("section", None, "seq"),
        ),
        check_vma=False,
    )
```

```python
import functools

import jax
import jax.numpy as jnp
from jax import lax
from jax.experimental import pallas as pl
from jax.experimental.pallas import tpu as pltpu
from jax.sharding import PartitionSpec as P

BASE_DILATION = 32
MARGIN = 2 * BASE_DILATION
GELU = 0.7978845608028654
CUBIC = 0.044715
MESH = pl.DeviceIdType.MESH
F32 = jnp.float32
BF16 = jnp.bfloat16
TN = (((0,), (0,)), ((), ()))


def gelu_pair(z):
    square = z * z
    t = jnp.tanh(z * (GELU + (GELU * CUBIC) * square))
    half = 0.5 + 0.5 * t
    value = z * half
    slope = half + (0.5 * z) * (1.0 - t * t) * (GELU + (3.0 * GELU * CUBIC) * square)
    return value, slope


def kernel(
    sizes,
    x_in,
    cot_in,
    cw_in,
    ow_in,
    ns_in,
    nb_in,
    is_in,
    ib_in,
    gin_ref,
    total_ref,
    x_ref,
    gtop,
    cw_ref,
    ow_ref,
    ns_ref,
    nb_ref,
    is_ref,
    ib_ref,
    cwt,
    owt,
    hid,
    gcv,
    slope_one,
    slope_two,
    inner,
    act,
    lhs,
    rhs,
    acc,
    row,
    yin,
    col,
    zin,
    load_sem,
    hid_send,
    hid_recv,
    gcv_send,
    gcv_recv,
    sec_send,
    sec_recv,
    lhs_send,
    lhs_recv,
    rhs_send,
    rhs_recv,
    y_send,
    y_recv,
    z_send,
    z_recv,
    all_send,
    all_recv,
):
    nx, ny, sections = sizes
    micros, rows, channels = x_ref.shape
    width = cw_ref.shape[2]
    half_c = channels // 2
    block = half_c // ny
    group = 2 * nx
    dp = lax.axis_index("dp")
    sec = lax.axis_index("section")
    seq = lax.axis_index("seq")
    x, core = dp // 2, dp % 2
    zh, y = seq // ny, seq % ny
    seqs = 2 * ny
    own = slice(MARGIN, MARGIN + rows)
    parity = sec % 2
    dil = BASE_DILATION * (1 + parity)
    has_prev, has_next = seq > 0, seq < seqs - 1
    is_top = sec == sections - 1
    not_top = sec < sections - 1
    is_low = sec == 0
    not_low = sec > 0

    def device(dp_at=dp, sec_at=sec, seq_at=seq):
        return (dp_at, sec_at, seq_at)

    def remote(src, dst, send, recv, to):
        return pltpu.make_async_remote_copy(
            src_ref=src,
            dst_ref=dst,
            send_sem=send,
            recv_sem=recv,
            device_id=to,
            device_id_type=MESH,
        )

    barrier = pltpu.get_barrier_semaphore()

    def greet(to):
        pl.semaphore_signal(barrier, inc=1, device_id=to, device_id_type=MESH)

    for step in range(1, group):
        greet(device(dp_at=lax.rem(dp + step, group)))
    for step in range(1, ny):
        greet(device(seq_at=zh * ny + lax.rem(y + step, ny)))
    greet(device(seq_at=(1 - zh) * ny + y))
    crosses_up = jnp.logical_and(zh == 0, y == ny - 1)
    crosses_down = jnp.logical_and(zh == 1, y == 0)
    pl.when(crosses_up)(lambda: greet(device(seq_at=seq + 1)))
    pl.when(crosses_down)(lambda: greet(device(seq_at=seq - 1)))
    pl.when(not_low)(lambda: greet(device(sec_at=sec - 1)))
    pl.when(not_top)(lambda: greet(device(sec_at=sec + 1)))
    expected = (
        group - 1 + ny - 1 + 1
        + jnp.where(crosses_up, 1, 0)
        + jnp.where(crosses_down, 1, 0)
        + jnp.where(not_low, 1, 0)
        + jnp.where(not_top, 1, 0)
    )

    def load(src, dst, i):
        return pltpu.make_async_copy(src, dst, load_sem.at[i])

    small = ((ns_in, ns_ref), (nb_in, nb_ref), (is_in, is_ref), (ib_in, ib_ref))

    def loads_small():
        return [load(src, dst, i) for i, (src, dst) in enumerate(small)]

    def load_x(m):
        return load(x_in.at[m], x_ref.at[m], 4 + m)

    def load_cw():
        return load(cw_in, cw_ref, 7)

    def load_ow():
        return load(ow_in, ow_ref, 8)

    def load_cot():
        return load(cot_in, gtop, 9)

    for copy in loads_small():
        copy.start()
    for m in range(micros):
        load_x(m).start()
    load_cw().start()
    load_ow().start()
    pl.when(is_top)(lambda: load_cot().start())

    def halo(buffer, m, send, recv, step):
        for par in range(2):
            d = BASE_DILATION * (1 + par)

            @pl.when(parity == par)
            def _():
                def up():
                    return remote(
                        buffer.at[m, pl.ds(MARGIN + rows - d, d)],
                        buffer.at[m, pl.ds(MARGIN - d, d)],
                        send.at[m, 0],
                        recv.at[m, 0],
                        device(seq_at=lax.rem(seq + 1, seqs)),
                    )

                def down():
                    return remote(
                        buffer.at[m, pl.ds(MARGIN, d)],
                        buffer.at[m, pl.ds(MARGIN + rows, d)],
                        send.at[m, 1],
                        recv.at[m, 1],
                        device(seq_at=lax.rem(seq + seqs - 1, seqs)),
                    )

                if step == "start":
                    pl.when(has_next)(lambda: up().start())
                    pl.when(has_prev)(lambda: down().start())
                elif step == "recv":
                    pl.when(has_prev)(lambda: up().wait_recv())
                    pl.when(has_next)(lambda: down().wait_recv())
                else:
                    pl.when(has_next)(lambda: up().wait_send())
                    pl.when(has_prev)(lambda: down().wait_send())

    for buffer in (hid, gcv):
        zero = jnp.zeros((micros, MARGIN, buffer.shape[2]), BF16)

        @pl.when(seq == 0)
        def _():
            buffer[:, :MARGIN] = zero

        @pl.when(seq == seqs - 1)
        def _():
            buffer[:, MARGIN + rows :] = zero

    tile = 32
    for copy in loads_small():
        copy.wait()

    for m in range(micros):
        load_x(m).wait()

        def activate(i, carry):
            at = pl.multiple_of(i * tile, tile)
            pre = x_ref[m, pl.ds(at, tile), :].astype(F32) * ns_ref[...] + nb_ref[...]
            value, slope = gelu_pair(pre)
            hid[m, pl.ds(MARGIN + at, tile), :] = value.astype(BF16)
            slope_one[m, pl.ds(at, tile), :] = slope * ns_ref[...]
            return carry

        lax.fori_loop(0, rows // tile, activate, 0)
        if m == 0:
            pl.semaphore_wait(barrier, expected)
        halo(hid, m, hid_send, hid_recv, "start")

    load_ow().wait()
    owt[...] = ow_ref[...].T
    load_cw().wait()
    for k in range(3):
        cwt[k] = cw_ref[k].T
    pl.when(is_top)(lambda: load_cot().wait())

    def tap_start(k, sign):
        return pl.multiple_of(MARGIN + sign * (k - 1) * dil, BASE_DILATION)

    def inner_forward(m):
        halo(hid, m, hid_send, hid_recv, "recv")
        total = None
        for k in range(3):
            term = jnp.dot(
                hid[m, pl.ds(tap_start(k, 1), rows), :], cw_ref[k], preferred_element_type=F32
            )
            total = term if total is None else total + term
        inner[...] = total

        def activate_inner(i, carry):
            at = pl.multiple_of(i * tile, tile)
            pre = inner[pl.ds(at, tile), :] * is_ref[...] + ib_ref[...]
            value, slope = gelu_pair(pre)
            act[m, pl.ds(at, tile), :] = value.astype(BF16)
            slope_two[m, pl.ds(at, tile), :] = slope * is_ref[...]
            return carry

        lax.fori_loop(0, rows // tile, activate_inner, 0)

    pieces = 3
    piece = channels // pieces

    def handed(m, n):
        cut = pl.ds(n * piece, piece)
        return remote(
            gin_ref.at[m, :, cut],
            gtop.at[m, :, cut],
            sec_send.at[m, n],
            sec_recv.at[m, n],
            device(sec_at=lax.rem(sec + sections - 1, sections)),
        )

    def input_grad(m, send):
        halo(gcv, m, gcv_send, gcv_recv, "recv")
        for n in range(pieces):
            cut = slice(n * piece, (n + 1) * piece)
            total = None
            for k in range(3):
                term = jnp.dot(
                    gcv[m, pl.ds(tap_start(k, -1), rows), :],
                    cwt[k, :, cut],
                    preferred_element_type=F32,
                )
                total = term if total is None else total + term
            gin_ref[m, :, cut] = (
                gtop[m, :, cut].astype(F32) + total * slope_one[m, :, cut]
            ).astype(BF16)
            if send:
                handed(m, n).start()

    steps = sorted(range(1, group), key=lambda t: -min(t, group - t))

    def peer(t):
        to = lax.rem(dp + t, group)
        return to, to // 2, lax.rem(to, 2)

    def half(c):
        return pl.ds(pl.multiple_of(c * half_c, 128), half_c)

    def lhs_tap(m, t):
        to, to_x, to_c = peer(t)
        return remote(
            hid.at[m, pl.ds(tap_start(to_x, 1), rows), half(to_c)],
            lhs.at[m, dp],
            lhs_send.at[m, t],
            lhs_recv.at[m, dp],
            device(dp_at=to),
        )

    def lhs_top(m, t):
        to, _, to_c = peer(t)
        return remote(
            gtop.at[m, :, half(to_c)],
            lhs.at[m, dp],
            lhs_send.at[m, t],
            lhs_recv.at[m, dp],
            device(dp_at=to),
        )

    def rhs_conv(m, t):
        to, _, _ = peer(t)
        return remote(
            gcv.at[m, pl.ds(MARGIN, rows)],
            rhs.at[m, dp],
            rhs_send.at[m, t],
            rhs_recv.at[m, dp],
            device(dp_at=to),
        )

    def rhs_act(m, t):
        to, _, _ = peer(t)
        return remote(
            act.at[m],
            rhs.at[m, dp],
            rhs_send.at[m, t],
            rhs_recv.at[m, dp],
            device(dp_at=to),
        )

    def exchange_early(m):
        for t in steps:
            _, to_x, _ = peer(t)
            pl.when(to_x < 3)(lambda: lhs_tap(m, t).start())
            pl.when(to_x == 3)(lambda: rhs_act(m, t).start())

    def exchange_late(m):
        for t in steps:
            _, to_x, _ = peer(t)
            pl.when(to_x < 3)(lambda: rhs_conv(m, t).start())
            pl.when(to_x == 3)(lambda: lhs_top(m, t).start())

    def weight_grad(m):
        @pl.when(x < 3)
        def _():
            lhs[m, dp] = hid[m, pl.ds(tap_start(x, 1), rows), half(core)]
            rhs[m, dp] = gcv[m, own, :]

        @pl.when(x == 3)
        def _():
            lhs[m, dp] = gtop[m, :, half(core)]
            rhs[m, dp] = act[m]

        for t in steps:
            source = lax.rem(dp + t, group)
            arrival = [
                remote(buffer.at[m, source], buffer.at[m, source], send.at[m, t], recv.at[m, source], device())
                for buffer, send, recv in ((lhs, lhs_send, lhs_recv), (rhs, rhs_send, rhs_recv))
            ]
            for copy in arrival:
                copy.wait_recv()
            if m == micros - 1:
                acc[...] += lax.dot_general(
                    lhs[m, source], rhs[m, source], TN, preferred_element_type=F32
                )
        if m == micros - 1:
            last = lax.dot_general(lhs[m, dp], rhs[m, dp], TN, preferred_element_type=F32)
            row[...] = (acc[...] + last).reshape(ny, block, width).astype(BF16)
            return
        term = lax.dot_general(
            lhs[m].reshape(group * rows, half_c),
            rhs[m].reshape(group * rows, width),
            TN,
            preferred_element_type=F32,
        )
        if m > 0:
            term = term + acc[...]
        if m < micros - 1:
            acc[...] = term
        else:
            row[...] = term.reshape(ny, block, width).astype(BF16)

    @pl.when(not_top)
    def _():
        for m in range(micros):
            inner_forward(m)
            exchange_early(m)

    for m in range(micros):

        @pl.when(is_top)
        def _():
            inner_forward(m)

        @pl.when(not_top)
        def _():
            for n in range(pieces):
                handed(m, n).wait_recv()

        grad_inner = jnp.dot(gtop[m], owt[...], preferred_element_type=F32)
        gcv[m, own, :] = (grad_inner * slope_two[m]).astype(BF16)
        halo(gcv, m, gcv_send, gcv_recv, "start")
        pl.when(is_top)(lambda: exchange_early(m))
        exchange_late(m)
        if m > 0:
            pl.when(not_low)(lambda: input_grad(m - 1, True))
    pl.when(not_low)(lambda: input_grad(micros - 1, True))

    weight_grad(0)

    @pl.when(is_low)
    def _():
        for m in range(micros - 1):
            input_grad(m, False)

    for m in range(1, micros):
        weight_grad(m)

    def y_copy(t):
        to = lax.rem(y + t, ny)
        return remote(
            row.at[to], yin.at[t], y_send.at[t], y_recv.at[t], device(seq_at=zh * ny + to)
        )

    far_first = sorted(range(1, ny), key=lambda t: -min(t, ny - t))
    for t in far_first:
        y_copy(t).start()

    pl.when(is_low)(lambda: input_grad(micros - 1, False))

    total = row[y].astype(F32)
    for t in reversed(far_first):
        y_copy(t).wait_recv()
        total = total + yin[t].astype(F32)
    col[...] = total.astype(BF16)

    def z_copy():
        return remote(col, zin, z_send.at[0], z_recv.at[0], device(seq_at=(1 - zh) * ny + y))

    def spread(t):
        return remote(
            total_ref.at[x],
            total_ref.at[x],
            all_send.at[t],
            all_recv.at[x],
            device(dp_at=lax.rem(dp + t, group)),
        )

    def arrival_of(k):
        return remote(total_ref.at[k], total_ref.at[k], all_send.at[0], all_recv.at[k], device())

    keeps = core == zh

    @pl.when(jnp.logical_not(keeps))
    def _():
        z_copy().start()

    @pl.when(keeps)
    def _():
        z_copy().wait_recv()
        total_ref[x] = (col[...].astype(F32) + zin[...].astype(F32)).astype(BF16)
        for t in steps:
            spread(t).start()

    for k in range(4):
        pl.when(jnp.logical_or(jnp.logical_not(keeps), x != k))(lambda: arrival_of(k).wait_recv())

    for m in range(micros):
        halo(hid, m, hid_send, hid_recv, "send")
        halo(gcv, m, gcv_send, gcv_recv, "send")

        @pl.when(not_low)
        def _():
            for n in range(pieces):
                handed(m, n).wait_send()

        for t in steps:
            lhs_top(m, t).wait_send()
            rhs_conv(m, t).wait_send()

    for t in far_first:
        y_copy(t).wait_send()

    @pl.when(jnp.logical_not(keeps))
    def _():
        z_copy().wait_send()

    @pl.when(keeps)
    def _():
        for t in steps:
            spread(t).wait_send()


def finish(factor, gin_in, total_in, gin_ref, gconv_ref, gout_ref):
    gin_ref[...] = gin_in[...]
    gconv_ref[...] = total_in[:3].astype(F32) * factor
    gout_ref[...] = total_in[3].astype(F32) * factor


def on_device(
    sizes,
    section_inputs,
    cotangent,
    conv_weight,
    out_weight,
    norm_scale,
    norm_shift,
    inner_scale,
    inner_shift,
):
    nx, ny, sections = sizes
    inputs = section_inputs[0, :, 0]
    micros, rows, channels = inputs.shape
    width = conv_weight.shape[3]
    half_c = channels // 2
    block = half_c // ny
    group = 2 * nx
    padded = rows + 2 * MARGIN
    dma = pltpu.SemaphoreType.DMA
    vmem = pl.BlockSpec(memory_space=pltpu.VMEM)
    anywhere = pl.BlockSpec(memory_space=pl.ANY)
    grad_in, total = pl.pallas_call(
        functools.partial(kernel, sizes),
        name="tower_backward",
        out_shape=(
            jax.ShapeDtypeStruct((micros, rows, channels), BF16),
            jax.ShapeDtypeStruct((4, block, width), BF16),
        ),
        in_specs=[anywhere] * 8,
        out_specs=(vmem, vmem),
        scratch_shapes=[
            pltpu.VMEM((micros, rows, channels), BF16),
            pltpu.VMEM((micros, rows, channels), BF16),
            pltpu.VMEM((3, channels, width), BF16),
            pltpu.VMEM((width, channels), BF16),
            pltpu.VMEM((1, channels), F32),
            pltpu.VMEM((1, channels), F32),
            pltpu.VMEM((1, width), F32),
            pltpu.VMEM((1, width), F32),
            pltpu.VMEM((3, width, channels), BF16),
            pltpu.VMEM((channels, width), BF16),
            pltpu.VMEM((micros, padded, channels), BF16),
            pltpu.VMEM((micros, padded, width), BF16),
            pltpu.VMEM((micros, rows, channels), F32),
            pltpu.VMEM((micros, rows, width), F32),
            pltpu.VMEM((rows, width), F32),
            pltpu.VMEM((micros, rows, width), BF16),
            pltpu.VMEM((micros, group, rows, half_c), BF16),
            pltpu.VMEM((micros, group, rows, width), BF16),
            pltpu.VMEM((half_c, width), F32),
            pltpu.VMEM((ny, block, width), BF16),
            pltpu.VMEM((ny, block, width), BF16),
            pltpu.VMEM((block, width), BF16),
            pltpu.VMEM((block, width), BF16),
            dma((10,)),
            dma((micros, 2)),
            dma((micros, 2)),
            dma((micros, 2)),
            dma((micros, 2)),
            dma((micros, 3)),
            dma((micros, 3)),
            dma((micros, group)),
            dma((micros, group)),
            dma((micros, group)),
            dma((micros, group)),
            dma((ny,)),
            dma((ny,)),
            dma((1,)),
            dma((1,)),
            dma((group,)),
            dma((4,)),
        ],
        compiler_params=pltpu.CompilerParams(
            collective_id=0, has_side_effects=True, vmem_limit_bytes=56 * 1024 * 1024
        ),
    )(
        inputs,
        cotangent[:, 0],
        conv_weight[0],
        out_weight[0],
        norm_scale,
        norm_shift,
        inner_scale,
        inner_shift,
    )
    grad_in, grad_conv, grad_out = pl.pallas_call(
        functools.partial(finish, 1.0 / float(micros * group)),
        name="write_results",
        out_shape=(
            jax.ShapeDtypeStruct((micros, rows, channels), BF16),
            jax.ShapeDtypeStruct((3, block, width), F32),
            jax.ShapeDtypeStruct((block, width), F32),
        ),
        in_specs=[vmem] * 2,
        out_specs=(vmem,) * 3,
    )(grad_in, total)
    return (
        grad_in.reshape(section_inputs.shape),
        grad_conv[None],
        grad_out.T[None],
    )


def solution(mesh):
    sizes = (mesh.shape["dp"] // 2, mesh.shape["seq"] // 2, mesh.shape["section"])
    return jax.shard_map(
        functools.partial(on_device, sizes),
        mesh=mesh,
        in_specs=(
            P("section", None, "dp", "seq", None),
            P(None, "dp", "seq", None),
            P("section", None, None, None),
            P("section", None, None),
            P("section", None),
            P("section", None),
            P("section", None),
            P("section", None),
        ),
        out_specs=(
            P("section", None, "dp", "seq", None),
            P("section", None, "seq", None),
            P("section", None, "seq"),
        ),
        check_vma=False,
    )
```
